32 devices in a mesh: tile: 16 (over z, y, x), spec: 2 (over core).
Axes of the slice: x: 2, y: 2, z: 4, core: 2. Of those that a mesh axis runs over, the one named last changes fastest.
Arguments:
- tracers: float32 [48, 2, 2048, 128], P('spec', None, 'tile'), may hold values from 0.1 to 10
- courant: float32 [2, 2, 2, 2, 2048, 128], P('spec', None, None, None, 'tile'), may hold values from -0.4 to 0.4
- diffusivity: float32 [2, 2, 2, 2, 2048, 128], P('spec', None, None, None, 'tile'), may hold values from 0.005 to 0.08
- edge_blocks: int32 [16, 4], P('tile'), may hold values from 0 to 15, as said below
- edge_flips: int32 [16, 4], P('tile'), may hold values from 0 to 1, as said below
- roots: int32 [2, 16], P(None, 'tile'), may hold values from 0 to 1
Outputs:
- transported: float32 [48, 2, 2048, 128], P('spec', None, 'tile')
The draws below stay inside these ranges and needn't reach their ends.
Inputs may be any that keep to these rules, and one draw needn't show every extreme that they name: `edge_blocks`: entries 0 to 3 of a row are the blocks across the west, east, south and north edges; if a is across b's east (north) edge then b is across a's west (south) edge; no block is across its own edge and the four blocks of a row differ. `edge_flips`: the flag of an edge equals the flag of the same edge seen from the block across it.
All inputs are finite; a program needn't handle non-finite values.
Results may differ from the reference program's by a relative error of at most 0.0003.
Values sent between devices are 32-bit elements; how exact they have to be, the bound alone decides.
A program may use at most 64 MiB of HBM per device.

```python
import math
import jax
import jax.numpy as jnp
from jax import lax

SPECIES = 48
LEV = 2
CELLS = 128
SUBSTEPS = 2
BLOCKS = 16
N_SPEC = 2


def torus_links(key):
    side_len = math.isqrt(BLOCKS)
    ordering = jax.random.permutation(jax.random.fold_in(key, 11), BLOCKS).astype(jnp.int32)
    position = jnp.argsort(ordering, stable=True).astype(jnp.int32)
    row_at = position // side_len
    col_at = position % side_len
    west_pos = row_at * side_len + (col_at - 1) % side_len
    east_pos = row_at * side_len + (col_at + 1) % side_len
    south_pos = (row_at - 1) % side_len * side_len + col_at
    north_pos = (row_at + 1) % side_len * side_len + col_at
    linked = jnp.stack([ordering[west_pos], ordering[east_pos], ordering[south_pos], ordering[north_pos]], 1).astype(jnp.int32)
    across = jax.random.randint(jax.random.fold_in(key, 23), (BLOCKS,), 0, 2, dtype=jnp.int32)
    upward = jax.random.randint(jax.random.fold_in(key, 29), (BLOCKS,), 0, 2, dtype=jnp.int32)
    turned = jnp.stack([across[west_pos], across[position], upward[south_pos], upward[position]], 1).astype(jnp.int32)
    return (linked, turned)


def draw_edge_blocks(key, part):
    return torus_links(key)[0]


def draw_edge_flips(key, part):
    return torus_links(key)[1]


def touch_ends(result, stream_key, low, top_value):
    index_at = [jax.random.randint(jax.random.fold_in(stream_key, axis), (), 0, length) for axis, length in enumerate(result.shape)]
    longest = result.shape.index(max(result.shape))
    beside = index_at[:longest] + [(index_at[longest] + 1) % result.shape[longest]] + index_at[longest + 1:]
    return result.at[tuple(index_at)].set(low).at[tuple(beside)].set(top_value)


def steps_of(key, extent, split, smallest, top_value):
    gain, own = 1.0, jax.random.fold_in(key, 6)
    for dim, parts in split:
        heights = jnp.exp(jax.random.uniform(jax.random.fold_in(own, dim), (parts,), jnp.float32, smallest / len(split), top_value / len(split)))
        gain = gain * jnp.repeat(heights, extent[dim] // parts).reshape([-1 if axis == dim else 1 for axis in range(len(extent))])
    return gain


def setup_inputs(seed: int = 0) -> dict:
    seeds = jax.random.split(jax.random.key(seed), 7)
    tracers = jnp.clip(jnp.exp(math.log(10.0) - 4.6051702 * jax.random.uniform(seeds[0], (SPECIES, LEV, BLOCKS * CELLS, CELLS), jnp.float32) ** steps_of(seeds[0], (SPECIES, LEV, BLOCKS * CELLS, CELLS), ((0, 2), (2, 16)), -0.2, 0.2)), 0.1, 10.0)
    courant = jnp.clip(jax.random.uniform(seeds[1], (N_SPEC, SUBSTEPS, 2, LEV, BLOCKS * CELLS, CELLS), jnp.float32, -0.4, 0.4) * steps_of(seeds[1], (N_SPEC, SUBSTEPS, 2, LEV, BLOCKS * CELLS, CELLS), ((0, 2), (4, 16)), -0.4, 0.0), -0.4, 0.4)
    diffusivity = jnp.clip(jnp.exp(math.log(0.08) - 2.7725887 * jax.random.uniform(seeds[2], (N_SPEC, SUBSTEPS, 2, LEV, BLOCKS * CELLS, CELLS), jnp.float32) ** steps_of(seeds[2], (N_SPEC, SUBSTEPS, 2, LEV, BLOCKS * CELLS, CELLS), ((0, 2), (4, 16)), -0.2, 0.2)), 0.005, 0.08)
    edge_blocks = draw_edge_blocks(jax.random.fold_in(seeds[6], 71), 0)
    edge_flips = draw_edge_flips(jax.random.fold_in(seeds[6], 71), 0)
    roots = touch_ends(jax.random.randint(seeds[5], (SUBSTEPS, BLOCKS), 0, N_SPEC), jax.random.fold_in(seeds[5], 1), 0, N_SPEC - 1).astype(jnp.int32)
    return {"tracers": tracers, "courant": courant, "diffusivity": diffusivity, "edge_blocks": edge_blocks, "edge_flips": edge_flips, "roots": roots}


def face_flux(padded, speed, kappa, along):
    inner = padded.shape[along] - 6

    def take_part(array, begin_at, end_at):
        return lax.slice_in_dim(array, begin_at, end_at, axis=along)

    edge_vals = (7.0 / 12.0) * (take_part(padded, 1, inner + 4) + take_part(padded, 2, inner + 5)) - (1.0 / 12.0) * (take_part(padded, 0, inner + 3) + take_part(padded, 3, inner + 6))
    lower_face = take_part(edge_vals, 0, inner + 1)
    centre = take_part(edge_vals, 1, inner + 2)
    upper_face = take_part(edge_vals, 2, inner + 3)
    behind = take_part(padded, 2, inner + 3)
    ahead_cell = take_part(padded, 3, inner + 4)
    reverse = -speed
    shape_pos = 6.0 * behind - 3.0 * (lower_face + centre)
    from_behind = centre - 0.5 * speed * ((centre - lower_face) - (1.0 - (2.0 / 3.0) * speed) * shape_pos)
    shape_neg = 6.0 * ahead_cell - 3.0 * (centre + upper_face)
    from_ahead = centre + 0.5 * reverse * ((upper_face - centre) + (1.0 - (2.0 / 3.0) * reverse) * shape_neg)
    face_val = jnp.where(speed > 0.0, from_behind, from_ahead)
    return speed * face_val - kappa * (ahead_cell - behind)


def edge_strips(field):
    west_side = jnp.swapaxes(field[..., :, 0:3], -1, -2)
    east_side = jnp.swapaxes(field[..., :, ::-1][..., :, 0:3], -1, -2)
    south_side = field[..., 0:3, :]
    north_side = field[..., ::-1, :][..., 0:3, :]
    return jnp.stack([west_side, east_side, south_side, north_side], 0)


def orient(strip_in, flipped):
    return jnp.where(flipped == 1, strip_in[..., ::-1], strip_in)


def advance(field, speed_x, speed_y, kappa_x, kappa_y, from_west, from_east, from_south, from_north, east_speed, east_kappa, north_speed, north_kappa):
    padded_x = jnp.concatenate([jnp.swapaxes(from_west[..., ::-1, :], -1, -2), field, jnp.swapaxes(from_east, -1, -2)], -1)
    padded_y = jnp.concatenate([from_south[..., ::-1, :], field, from_north], -2)
    faces_cx = jnp.concatenate([speed_x, east_speed[..., None]], -1)
    faces_kx = jnp.concatenate([kappa_x, east_kappa[..., None]], -1)
    faces_cy = jnp.concatenate([speed_y, north_speed[..., None, :]], -2)
    faces_ky = jnp.concatenate([kappa_y, north_kappa[..., None, :]], -2)
    flux_x = face_flux(padded_x, faces_cx, faces_kx, padded_x.ndim - 1)
    flux_y = face_flux(padded_y, faces_cy, faces_ky, padded_y.ndim - 2)
    return field - (flux_x[..., 1:] - flux_x[..., :-1]) - (flux_y[..., 1:, :] - flux_y[..., :-1, :])


def substep_all(field, speeds, kappas, neighbours, flips):
    strips = edge_strips(field)

    def fetch(source, edge):
        got = jnp.take(strips[source], neighbours[:, edge], axis=1)
        return orient(got, flips[:, edge][None, :, None, None])

    def face_fetch(values, edge):
        got = jnp.take(values, neighbours[:, edge], axis=1)
        return orient(got, flips[:, edge][None, :, None])

    east_speed = face_fetch(speeds[0][..., :, 0], 1)
    east_kappa = face_fetch(kappas[0][..., :, 0], 1)
    north_speed = face_fetch(speeds[1][..., 0, :], 3)
    north_kappa = face_fetch(kappas[1][..., 0, :], 3)
    return advance(field, speeds[0], speeds[1], kappas[0], kappas[1], fetch(1, 0), fetch(0, 1), fetch(3, 2), fetch(2, 3), east_speed, east_kappa, north_speed, north_kappa)


def pick_member(source, chosen):
    members = source.reshape(source.shape[0], 2, LEV, BLOCKS, CELLS, CELLS)
    index = chosen.astype(jnp.int32)[None, None, None, :, None, None]
    index = jnp.broadcast_to(index, (1, 2, LEV, BLOCKS, CELLS, CELLS))
    return jnp.take_along_axis(members, index, axis=0)[0]


def reference(tracers, courant, diffusivity, edge_blocks, edge_flips, roots):
    blocks_all = tracers.reshape(SPECIES, LEV, BLOCKS, CELLS, CELLS)
    fields = []
    for substep in range(SUBSTEPS):
        speeds = pick_member(courant[:, substep], roots[substep])
        kappas = pick_member(diffusivity[:, substep], roots[substep])
        fields.append((speeds, kappas))

    def one_species(field):
        for speeds, kappas in fields:
            field = substep_all(field, speeds, kappas, edge_blocks, edge_flips)
        return field

    moved = lax.map(one_species, blocks_all)
    return moved.reshape(SPECIES, LEV, BLOCKS * CELLS, CELLS)
```

```python
import functools

import jax
import jax.numpy as jnp
from jax import lax
from jax.experimental import pallas as pl
from jax.experimental.pallas import tpu as pltpu
from jax.sharding import PartitionSpec as P

MESH = pl.DeviceIdType.MESH
C = 128
PITCH = 144
FPITCH = C + 8
VMEM_LIMIT = 56 * 1024 * 1024
SHIFTS = (-3, -2, -1, 0, 1, 2, 3)
DATA_EDGES = ((0, 1), (1, 0), (2, 3), (3, 2))
FACE_EDGES = ((1, 0), (3, 2))


def taps(c, k):
    s = jnp.abs(c)
    rest = 1.0 - s
    mid = c * rest * rest
    outer = -s * rest
    ahead = (3.0 - 2.0 * s) * s
    pos = jnp.maximum(c, 0.0)
    neg = jnp.minimum(c, 0.0)
    out_pos = pos * outer
    out_neg = neg * outer
    a = 7.0 / 12.0
    b = -1.0 / 12.0
    return [
        b * out_pos,
        b * mid + a * out_pos,
        a * (mid + out_pos) + b * out_neg + pos * ahead + k,
        a * (mid + out_neg) + b * out_pos + neg * ahead - k,
        b * mid + a * out_neg,
        b * out_neg,
    ]


def stencil(low, high):
    lo = low + [None]
    hi = [None] + high
    return [-b if a is None else a if b is None else a - b for a, b in zip(lo, hi)]


class Plan:
    def __init__(self, sizes, species):
        n = sizes["tile"]
        self.members = sizes["spec"]
        self.m = 4
        rest = n // self.m
        self.b = 1
        while self.b * self.b * 4 <= rest:
            self.b *= 2
        self.a = rest // self.b
        self.sc = max(d for d in range(1, 9) if species % d == 0)
        self.nch = 2 * (species // self.sc)
        self.nu = 2 * self.nch
        self.d1, self.d2, self.d3 = 2, 4, 6
        self.period = max(self.nch, self.d3)
        self.ticks = self.period + self.nch + self.d3
        assert self.a * self.b * self.m == n


class Here:
    def __init__(self, p):
        self.p = p
        me = lax.axis_index("tile")
        self.mate = lax.rem(me, p.m)
        self.low = lax.rem(me // p.m, p.b)
        self.far = me // (p.m * p.b)

    def at(self, far=0, low=0, mate=0):
        p = self.p
        f = lax.rem(self.far + (far + p.a), p.a)
        w = lax.rem(self.low + (low + p.b), p.b)
        i = lax.rem(self.mate + (mate + p.m), p.m)
        return (f * p.b + w) * p.m + i


def remote(src, dst, send, recv, tile):
    return pltpu.make_async_remote_copy(
        src_ref=src,
        dst_ref=dst,
        send_sem=send,
        recv_sem=recv,
        device_id={"tile": tile},
        device_id_type=MESH,
    )


class Swap:
    def __init__(self, p, here, edges, rows, bufs, sems, meta):
        self.p, self.here, self.edges, self.rows, self.meta = p, here, edges, rows, meta
        self.raw, self.s2, self.r2, self.s3, self.r3 = bufs
        self.send, self.recv = sems
        p = self.p
        self.at_2a = p.a - 1
        self.at_2b = self.at_2a + p.m - 1
        self.at_3 = self.at_2b + p.m - 1

    def first(self, u, off):
        return remote(
            self.raw.at[u, 0], self.raw.at[u, off], self.send.at[u, off - 1],
            self.recv.at[u, off - 1], self.here.at(far=off),
        )

    def own_slots(self, u, off):
        i = self.at_2a + off - 1
        return remote(
            self.s2.at[u, off - 1, 0], self.r2.at[u, off - 1, 0], self.send.at[u, i],
            self.recv.at[u, i], self.here.at(mate=off),
        )

    def far_slots(self, u, off):
        i = self.at_2b + off - 1
        part = pl.ds(1, self.p.a - 1)
        return remote(
            self.s2.at[u, off - 1, part], self.r2.at[u, off - 1, part], self.send.at[u, i],
            self.recv.at[u, i], self.here.at(mate=off),
        )

    def last(self, u, off):
        i = self.at_3 + off - 1
        return remote(
            self.s3.at[u, off - 1], self.r3.at[u, off - 1], self.send.at[u, i],
            self.recv.at[u, i], self.here.at(low=off),
        )

    def wanted(self, which, edge):
        return jnp.broadcast_to(self.meta[which, pl.ds(edge, 1), :], (8, C))

    def fill(self, u, source):
        p, here = self.p, self.here
        rows = [self.wanted(source, src) for _, src in self.edges]
        index = [j for j in range(len(self.edges))]
        slot_of = {src: j for j, (_, src) in enumerate(sorted(self.edges, key=lambda x: x[1]))}
        for off in range(1, p.m):
            for low in range(p.b):
                dest = here.at(far=0, low=low, mate=off)
                masks = [row == dest for row in rows]
                for d in range(self.rows // 8):
                    part = pl.ds(8 * d, 8)
                    value = None
                    for j in index:
                        strip = self.raw[u, source, slot_of[self.edges[j][1]], part, :]
                        value = strip if value is None else jnp.where(masks[j], strip, value)
                    self.s2[u, off - 1, source, low, part, :] = value

    def start(self, u):
        p = self.p
        for off in range(1, p.a):
            self.first(u, off).start()
        self.fill(u, 0)
        for off in range(1, p.m):
            self.own_slots(u, off).start()

    def middle(self, u):
        p = self.p
        for off in range(1, p.a):
            self.first(u, off).wait_recv()
        for off in range(1, p.a):
            self.fill(u, off)
        for off in range(1, p.m):
            self.far_slots(u, off).start()

    def arrived(self, u, low, which):
        p, here = self.p, self.here
        slot_of = {src: j for j, (_, src) in enumerate(sorted(self.edges, key=lambda x: x[1]))}
        result = []
        for j, (dst, src) in enumerate(self.edges):
            want = self.wanted(which, dst)
            sources = []
            for far in range(p.a):
                if low or far:
                    ident = here.at(far=-far)
                    sources.append((want == ident, lambda part, far=far, slot=slot_of[src]: self.raw[u, far, slot, part, :]))
                for off in range(1, p.m):
                    ident = here.at(far=-far, mate=-off)
                    sources.append(
                        (want == ident, lambda part, far=far, off=off: self.r2[u, off - 1, far, low, part, :])
                    )
            result.append((want, sources))
        return result

    def late(self, u):
        p = self.p
        for off in range(1, p.m):
            self.own_slots(u, off).wait_recv()
            self.far_slots(u, off).wait_recv()
        for low in range(1, p.b):
            for j, (_, sources) in enumerate(self.arrived(u, low, p.a + low - 1)):
                for d in range(self.rows // 8):
                    part = pl.ds(8 * d, 8)
                    value = None
                    for mask, load in sources:
                        value = load(part) if value is None else jnp.where(mask, load(part), value)
                    self.s3[u, low - 1, j, part, :] = value
            self.last(u, low).start()

    def finish(self, u):
        p, here = self.p, self.here
        for off in range(1, p.b):
            self.last(u, off).wait_recv()
        strips = []
        for j, (want, sources) in enumerate(self.arrived(u, 0, 0)):
            column = lax.rem(lax.div(want, p.m), p.b)
            for off in range(1, p.b):
                ident = lax.rem(here.low + (p.b - off), p.b)
                sources.append((column == ident, lambda part, off=off: self.r3[u, off - 1, j, part, :]))
            for d in range(self.rows // 8):
                part = pl.ds(8 * d, 8)
                value = None
                for mask, load in sources:
                    value = load(part) if value is None else jnp.where(mask, load(part), value)
                strips.append(value)
        return strips

    def drain(self, u):
        p = self.p
        for off in range(1, p.a):
            self.first(u, off).wait_send()
        for off in range(1, p.m):
            self.own_slots(u, off).wait_send()
            self.far_slots(u, off).wait_send()
        for off in range(1, p.b):
            self.last(u, off).wait_send()


def reversed_lanes(x):
    row = lax.broadcasted_iota(jnp.int32, (C, C), 0)
    col = lax.broadcasted_iota(jnp.int32, (C, C), 1)
    turn = jnp.where(row + col == C - 1, 1.0, 0.0).astype(jnp.bfloat16)
    total = None
    for _ in range(3):
        piece = x.astype(jnp.bfloat16)
        x = x - piece.astype(jnp.float32)
        part = jnp.dot(piece, turn, preferred_element_type=jnp.float32)
        total = part if total is None else total + part
    return total


def kernel(
    p, near, flips, roots, q_in, cour, diff, out,
    q, qt, xs, fields, fpad, coef, meta,
    raw, s2, r2, s3, r3, fraw, fs2, fr2, fs3, fr3,
    send, recv, fsend, frecv, in_sem, out_sem, field_sem, spread_sem, meta_sem,
):
    here = Here(p)
    spec = lax.axis_index("spec")
    sc, nch = p.sc, p.nch

    def plane_in(c, s):
        row = pl.multiple_of((c * sc + s) * PITCH + 8, 8)
        return pltpu.make_async_copy(
            q_in.at[(c // 2) * sc + s, lax.rem(c, 2)], q.at[pl.ds(row, C), :], in_sem.at[c, s]
        )

    def plane_out(c, s):
        row = pl.multiple_of(((2 * nch + c) * sc + s) * PITCH + 8, 8)
        return pltpu.make_async_copy(
            q.at[pl.ds(row, C), :], out.at[(c // 2) * sc + s, lax.rem(c, 2)], out_sem.at[c, s]
        )

    @pl.loop(0, nch)
    def _(c):
        for s in range(sc):
            plane_in(c, s).start()

    own_fields = [
        pltpu.make_async_copy(src.at[0], fields.at[t, spec], field_sem.at[t])
        for t, src in enumerate((cour, diff))
    ]
    for copy in own_fields:
        copy.start()

    barrier = pltpu.get_barrier_semaphore()
    partners = [here.at(far=o) for o in range(1, p.a)]
    partners += [here.at(mate=o) for o in range(1, p.m)]
    partners += [here.at(low=o) for o in range(1, p.b)]
    for tile in partners:
        pl.semaphore_signal(barrier, inc=1, device_id={"tile": tile}, device_id_type=MESH)
    for off in range(1, p.members):
        peer = lax.rem(spec + off, p.members)
        pl.semaphore_signal(barrier, inc=1, device_id={"spec": peer}, device_id_type=MESH)

    edge_row = lax.broadcasted_iota(jnp.int32, (8, C), 0)
    tile = jnp.full((8, C), near[0, 3], jnp.int32)
    for e in range(3):
        tile = jnp.where(edge_row == e, near[0, e], tile)
    meta[0] = tile

    pl.semaphore_wait(barrier, len(partners) + p.members - 1)

    def spread(t, src, off):
        peer = lax.rem(spec + off, p.members)
        return pltpu.make_async_remote_copy(
            src_ref=src.at[0],
            dst_ref=fields.at[t, spec],
            send_sem=spread_sem.at[0, t, off],
            recv_sem=spread_sem.at[1, t, off],
            device_id={"spec": peer},
            device_id_type=MESH,
        )

    spreads = [
        spread(t, src, off) for off in range(1, p.members) for t, src in enumerate((cour, diff))
    ]
    metas = [
        remote(meta.at[0], meta.at[o], meta_sem.at[0, o], meta_sem.at[1, o], here.at(far=o))
        for o in range(1, p.a)
    ]
    metas += [
        remote(
            meta.at[0], meta.at[p.a + o - 1], meta_sem.at[0, p.a + o - 1],
            meta_sem.at[1, p.a + o - 1], here.at(low=-o),
        )
        for o in range(1, p.b)
    ]
    for copy in metas + spreads:
        copy.start()

    data = Swap(p, here, DATA_EDGES, 24, (raw, s2, r2, s3, r3), (send, recv), meta)
    face = Swap(p, here, FACE_EDGES, 8, (fraw, fs2, fr2, fs3, fr3), (fsend, frecv), meta)

    def transpose_planes(src, src_base, src_pitch, dst, dst_base, dst_pitch):
        for s in range(sc):
            a = pl.multiple_of(src_base + s * src_pitch, 8)
            b = pl.multiple_of(dst_base + s * dst_pitch, 8)
            dst[pl.ds(b, C), :] = src[pl.ds(a, C), :].T

    def pack(u):
        base = u * (sc * PITCH) + 8
        strips = []
        for ref, first in ((qt, 0), (qt, C - 1), (q, 0), (q, C - 1)):
            for d in range(3):
                at = first + d if first == 0 else first - d
                strip = ref[pl.ds(base + at, sc, stride=PITCH), :]
                if sc < 8:
                    strip = jnp.concatenate([strip, jnp.zeros((8 - sc, C), jnp.float32)], 0)
                strips.append(strip)
        turned = reversed_lanes(jnp.concatenate(strips, 0))
        for e in range(4):
            flipped = jnp.full((8, C), flips[0, e], jnp.int32) == 1
            for d in range(3):
                i = 3 * e + d
                raw[u, 0, e, pl.ds(8 * d, 8), :] = jnp.where(
                    flipped, turned[8 * i : 8 * i + 8], strips[i]
                )

    def prepare_fields():
        for copy in own_fields:
            copy.wait()
        for copy in spreads:
            copy.wait_recv()
        for t in range(2):
            for k in range(2):
                root = roots[0, k]
                for lev in range(2):
                    at = ((k * 2 + t) * 2 + lev) * FPITCH
                    fpad[0, pl.ds(at, C), :] = fields[t, root, k, 0, lev].T
                    fpad[1, pl.ds(at, C), :] = fields[t, root, k, 1, lev]

    def pack_faces():
        for i, e in enumerate((0, 2)):
            tile = fpad[i, pl.ds(0, 8, stride=FPITCH), :]
            flipped = jnp.full((8, C), flips[0, e], jnp.int32) == 1
            fraw[0, 0, i] = jnp.where(flipped, reversed_lanes(tile), tile)

    def end_faces():
        for i, tile in enumerate(face.finish(0)):
            fpad[i, pl.ds(C, 8, stride=FPITCH), :] = tile

    def coefficients(k):
        @pl.loop(0, C // 8)
        def _(r):
            at = pl.multiple_of(r * 8, 8)
            for lev in range(2):
                for way in range(2):
                    low, high = [], []
                    for t in range(2):
                        base = ((k * 2 + t) * 2 + lev) * FPITCH + at
                        low.append(fpad[way, pl.ds(pl.multiple_of(base, 8), 8), :])
                        high.append(fpad[way, pl.ds(base + 1, 8), :])
                    values = stencil(taps(*low), taps(*high))
                    if way == 1:
                        values[3] = values[3] + 1.0
                    for i, value in enumerate(values):
                        coef[k * 2 + lev, way * 7 + i, pl.ds(at, 8), :] = value

    def compute(k, c):
        u = k * nch + c
        which = k * 2 + lax.rem(c, 2)
        base = u * (sc * PITCH)
        nxt = (u + nch) * (sc * PITCH)
        strips = data.finish(u)
        for e, (ref, low) in enumerate(((qt, True), (qt, False), (q, True), (q, False))):
            for d in range(3):
                at = base + (7 - d if low else C + 8 + d)
                ref[pl.ds(at, sc, stride=PITCH), :] = strips[3 * e + d][:sc]

        @pl.loop(0, C // 8)
        def _(r):
            at = pl.multiple_of(r * 8, 8)
            w = [coef[which, i, pl.ds(at, 8), :] for i in range(7)]
            for s in range(sc):
                row = base + (s * PITCH + 8) + at
                total = None
                for i, d in enumerate(SHIFTS):
                    term = w[i] * qt[pl.ds(row + d, 8), :]
                    total = term if total is None else total + term
                xs[pl.ds(pl.multiple_of(s * C + at, 8), 8), :] = total

        transpose_planes(xs, 0, C, q, nxt + 8, PITCH)

        @pl.loop(0, C // 8)
        def _(r):
            at = pl.multiple_of(r * 8, 8)
            w = [coef[which, 7 + i, pl.ds(at, 8), :] for i in range(7)]
            for s in range(sc):
                row = base + (s * PITCH + 8) + at
                block = pl.ds(pl.multiple_of(nxt + (s * PITCH + 8) + at, 8), 8)
                total = q[block, :]
                for i, d in enumerate(SHIFTS):
                    total += w[i] * q[pl.ds(row + d, 8), :]
                q[block, :] = total

    def staged(t, delay):
        at = t - delay
        k = at // p.period
        c = at - k * p.period
        return k, c, (at >= 0) & (k < 2) & (c < nch)

    face_at = min(1, nch - 1)

    @pl.loop(0, p.ticks)
    def _(t):
        @pl.when(t < nch)
        def _():
            for s in range(sc):
                plane_in(t, s).wait()
            base = t * (sc * PITCH) + 8
            transpose_planes(q, base, PITCH, qt, base, PITCH)
            pack(t)
            data.start(t)

        @pl.when(t == face_at)
        def _():
            prepare_fields()
            pack_faces()
            face.start(0)

        k3, c3, on3 = staged(t, p.d2)

        @pl.when(t == p.d1)
        def _():
            for copy in metas:
                copy.wait_recv()

        @pl.when(t == face_at + p.d2)
        def _():
            face.late(0)

        @pl.when(on3)
        def _():
            data.late(k3 * nch + c3)

        k2, c2, on2 = staged(t, p.d1)

        @pl.when(on2)
        def _():
            data.middle(k2 * nch + c2)

        @pl.when(t == face_at + p.d1)
        def _():
            face.middle(0)

        @pl.when(t == p.d3)
        def _():
            end_faces()
            coefficients(0)
            coefficients(1)

        k4, c4, on4 = staged(t, p.d3)

        @pl.when(on4)
        def _():
            compute(k4, c4)

            @pl.when(k4 == 0)
            def _():
                base = (nch + c4) * (sc * PITCH) + 8
                transpose_planes(q, base, PITCH, qt, base, PITCH)
                pack(nch + c4)
                data.start(nch + c4)

            @pl.when(k4 == 1)
            def _():
                for s in range(sc):
                    plane_out(c4, s).start()

    for copy in metas + spreads:
        copy.wait_send()
    face.drain(0)

    @pl.loop(0, p.nu)
    def _(u):
        data.drain(u)

    @pl.loop(0, nch)
    def _(c):
        for s in range(sc):
            plane_out(c, s).wait()


def body(sizes, tracers, courant, diffusivity, edge_blocks, edge_flips, roots):
    p = Plan(sizes, tracers.shape[0])
    anywhere = pl.BlockSpec(memory_space=pl.ANY)
    scalars = pl.BlockSpec(memory_space=pltpu.SMEM)
    f32 = jnp.float32
    planes = p.nch * p.sc
    count = p.a - 1 + 2 * (p.m - 1) + p.b - 1

    def buffers(nu, edges, rows):
        return [
            pltpu.VMEM((nu, p.a, edges, rows, C), f32),
            pltpu.VMEM((nu, p.m - 1, p.a, p.b, rows, C), f32),
            pltpu.VMEM((nu, p.m - 1, p.a, p.b, rows, C), f32),
            pltpu.VMEM((nu, p.b - 1, edges, rows, C), f32),
            pltpu.VMEM((nu, p.b - 1, edges, rows, C), f32),
        ]

    dma = pltpu.SemaphoreType.DMA
    return pl.pallas_call(
        functools.partial(kernel, p),
        out_shape=jax.ShapeDtypeStruct(tracers.shape, tracers.dtype),
        in_specs=[scalars] * 3 + [anywhere] * 3,
        out_specs=anywhere,
        scratch_shapes=[
            pltpu.VMEM((3 * planes * PITCH, C), f32),
            pltpu.VMEM((2 * planes * PITCH, C), f32),
            pltpu.VMEM((p.sc * C, C), f32),
            pltpu.VMEM((2, p.members, 2, 2, 2, C, C), f32),
            pltpu.VMEM((2, 8 * FPITCH, C), f32),
            pltpu.VMEM((4, 14, C, C), f32),
            pltpu.VMEM((p.a + p.b - 1, 8, C), jnp.int32),
            *buffers(p.nu, 4, 24),
            *buffers(1, 2, 8),
            dma((p.nu, count)),
            dma((p.nu, count)),
            dma((1, count)),
            dma((1, count)),
            dma((p.nch, p.sc)),
            dma((p.nch, p.sc)),
            dma((2,)),
            dma((2, 2, p.members)),
            dma((2, p.a + p.b - 1)),
        ],
        compiler_params=pltpu.CompilerParams(
            collective_id=0, has_side_effects=True, vmem_limit_bytes=VMEM_LIMIT
        ),
        name="transport",
    )(edge_blocks, edge_flips, roots.reshape(1, 2), tracers, courant, diffusivity)


def solution(mesh):
    placed = (
        P("spec", None, "tile", None),
        P("spec", None, None, None, "tile", None),
        P("spec", None, None, None, "tile", None),
        P("tile", None),
        P("tile", None),
        P(None, "tile"),
    )
    return jax.shard_map(
        functools.partial(body, dict(mesh.shape)),
        mesh=mesh,
        in_specs=placed,
        out_specs=P("spec", None, "tile", None),
        check_vma=False,
    )
```

```python
import functools

import jax
import jax.numpy as jnp
from jax import lax
from jax.experimental import pallas as pl
from jax.experimental.pallas import tpu as pltpu
from jax.sharding import PartitionSpec as P

MESH = pl.DeviceIdType.MESH
C = 128
PITCH = 144
FPITCH = C + 8
VMEM_LIMIT = 56 * 1024 * 1024
SHIFTS = (-3, -2, -1, 0, 1, 2, 3)
DATA_EDGES = ((0, 1), (1, 0), (2, 3), (3, 2))
FACE_EDGES = ((1, 0), (3, 2))


def taps(c, k):
    s = jnp.abs(c)
    rest = 1.0 - s
    mid = c * rest * rest
    outer = -s * rest
    ahead = (3.0 - 2.0 * s) * s
    pos = jnp.maximum(c, 0.0)
    neg = jnp.minimum(c, 0.0)
    out_pos = pos * outer
    out_neg = neg * outer
    a = 7.0 / 12.0
    b = -1.0 / 12.0
    return [
        b * out_pos,
        b * mid + a * out_pos,
        a * (mid + out_pos) + b * out_neg + pos * ahead + k,
        a * (mid + out_neg) + b * out_pos + neg * ahead - k,
        b * mid + a * out_neg,
        b * out_neg,
    ]


def stencil(low, high):
    lo = low + [None]
    hi = [None] + high
    return [-b if a is None else a if b is None else a - b for a, b in zip(lo, hi)]


class Plan:
    def __init__(self, sizes, species):
        n = sizes["tile"]
        self.members = sizes["spec"]
        self.m = 4
        rest = n // self.m
        self.b = 1
        while self.b * self.b * 4 <= rest:
            self.b *= 2
        self.a = rest // self.b
        self.sc = max(d for d in range(1, 9) if species % d == 0)
        self.nch = 2 * (species // self.sc)
        self.nu = 2 * self.nch
        self.late, self.end, self.turn = 2, 4, 3
        self.face_middle, self.face_late = 1, 3
        self.period = max(self.nch, self.end + self.turn)
        self.ticks = self.period + self.nch + self.end
        assert self.a == self.b and self.a * self.b * self.m == n


class Here:
    def __init__(self, p, swapped):
        self.p, self.swapped = p, swapped
        me = lax.axis_index("tile")
        self.mate = lax.rem(me, p.m)
        low = lax.rem(me // p.m, p.b)
        far = me // (p.m * p.b)
        self.first = far + swapped * (low - far)
        self.last = low + swapped * (far - low)
        self.first_stride = p.m * (p.b + swapped * (1 - p.b))
        self.last_stride = p.m * (1 + swapped * (p.b - 1))

    def at(self, first=0, last=0, mate=0):
        p = self.p
        f = lax.rem(self.first + (first + p.a), p.a)
        w = lax.rem(self.last + (last + p.b), p.b)
        i = lax.rem(self.mate + (mate + p.m), p.m)
        return f * self.first_stride + w * self.last_stride + i

    def near_of_source(self, off):
        return off if off == 0 else off + self.swapped * (self.p.a - 1)

    def near_of_target(self, off):
        return self.p.b - off + (1 - self.swapped) * (self.p.a - 1)


def remote(src, dst, send, recv, tile):
    return pltpu.make_async_remote_copy(
        src_ref=src,
        dst_ref=dst,
        send_sem=send,
        recv_sem=recv,
        device_id={"tile": tile},
        device_id_type=MESH,
    )


class Swap:
    def __init__(self, p, here, edges, rows, bufs, sems, meta):
        self.p, self.here, self.edges, self.rows, self.meta = p, here, edges, rows, meta
        self.raw, self.s2, self.r2, self.s3, self.r3 = bufs
        self.send, self.recv = sems
        p = self.p
        self.at_2a = p.a - 1
        self.at_2b = self.at_2a + p.m - 1
        self.at_3 = self.at_2b + p.m - 1

    def first(self, u, off):
        return remote(
            self.raw.at[u, 0], self.raw.at[u, off], self.send.at[u, off - 1],
            self.recv.at[u, off - 1], self.here.at(first=off),
        )

    def own_slots(self, u, off):
        i = self.at_2a + off - 1
        return remote(
            self.s2.at[u, off - 1, 0], self.r2.at[u, off - 1, 0], self.send.at[u, i],
            self.recv.at[u, i], self.here.at(mate=off),
        )

    def far_slots(self, u, off):
        i = self.at_2b + off - 1
        part = pl.ds(1, self.p.a - 1)
        return remote(
            self.s2.at[u, off - 1, part], self.r2.at[u, off - 1, part], self.send.at[u, i],
            self.recv.at[u, i], self.here.at(mate=off),
        )

    def last(self, u, off):
        i = self.at_3 + off - 1
        return remote(
            self.s3.at[u, off - 1], self.r3.at[u, off - 1], self.send.at[u, i],
            self.recv.at[u, i], self.here.at(last=off),
        )

    def wanted(self, which, edge):
        return jnp.broadcast_to(self.meta[which, pl.ds(edge, 1), :], (8, C))

    def fill(self, u, source):
        p, here = self.p, self.here
        rows = [self.wanted(here.near_of_source(source), src) for _, src in self.edges]
        index = [j for j in range(len(self.edges))]
        slot_of = {src: j for j, (_, src) in enumerate(sorted(self.edges, key=lambda x: x[1]))}
        for off in range(1, p.m):
            for low in range(p.b):
                dest = here.at(last=low, mate=off)
                masks = [row == dest for row in rows]
                for d in range(self.rows // 8):
                    part = pl.ds(8 * d, 8)
                    value = None
                    for j in index:
                        strip = self.raw[u, source, slot_of[self.edges[j][1]], part, :]
                        value = strip if value is None else jnp.where(masks[j], strip, value)
                    self.s2[u, off - 1, source, low, part, :] = value

    def start(self, u):
        p = self.p
        for off in range(1, p.a):
            self.first(u, off).start()
        self.fill(u, 0)
        for off in range(1, p.m):
            self.own_slots(u, off).start()

    def middle(self, u):
        p = self.p
        for off in range(1, p.a):
            self.first(u, off).wait_recv()
        for off in range(1, p.a):
            self.fill(u, off)
        for off in range(1, p.m):
            self.far_slots(u, off).start()

    def arrived(self, u, low, which):
        p, here = self.p, self.here
        slot_of = {src: j for j, (_, src) in enumerate(sorted(self.edges, key=lambda x: x[1]))}
        result = []
        for j, (dst, src) in enumerate(self.edges):
            want = self.wanted(which, dst)
            sources = []
            for far in range(p.a):
                if low or far:
                    ident = here.at(first=-far)
                    sources.append((want == ident, lambda part, far=far, slot=slot_of[src]: self.raw[u, far, slot, part, :]))
                for off in range(1, p.m):
                    ident = here.at(first=-far, mate=-off)
                    sources.append(
                        (want == ident, lambda part, far=far, off=off: self.r2[u, off - 1, far, low, part, :])
                    )
            result.append((want, sources))
        return result

    def late(self, u):
        p, here = self.p, self.here
        for off in range(1, p.m):
            self.own_slots(u, off).wait_recv()
            self.far_slots(u, off).wait_recv()
        for low in range(1, p.b):
            for j, (_, sources) in enumerate(self.arrived(u, low, here.near_of_target(low))):
                for d in range(self.rows // 8):
                    part = pl.ds(8 * d, 8)
                    value = None
                    for mask, load in sources:
                        value = load(part) if value is None else jnp.where(mask, load(part), value)
                    self.s3[u, low - 1, j, part, :] = value
            self.last(u, low).start()

    def finish(self, u):
        p, here = self.p, self.here
        for off in range(1, p.b):
            self.last(u, off).wait_recv()
        strips = []
        for j, (want, sources) in enumerate(self.arrived(u, 0, 0)):
            for off in range(1, p.b):
                column = self.column(want)
                ident = lax.rem(here.last + (p.b - off), p.b)
                sources.append((column == ident, lambda part, off=off: self.r3[u, off - 1, j, part, :]))
            for d in range(self.rows // 8):
                part = pl.ds(8 * d, 8)
                value = None
                for mask, load in sources:
                    value = load(part) if value is None else jnp.where(mask, load(part), value)
                strips.append(value)
        return strips

    def column(self, want):
        p, here = self.p, self.here
        near, far = lax.rem(lax.div(want, p.m), p.b), lax.div(want, p.m * p.b)
        return near + here.swapped * (far - near)

    def drain(self, u):
        p = self.p
        for off in range(1, p.a):
            self.first(u, off).wait_send()
        for off in range(1, p.m):
            self.own_slots(u, off).wait_send()
            self.far_slots(u, off).wait_send()
        for off in range(1, p.b):
            self.last(u, off).wait_send()


def reversed_lanes(x):
    row = lax.broadcasted_iota(jnp.int32, (C, C), 0)
    col = lax.broadcasted_iota(jnp.int32, (C, C), 1)
    turn = jnp.where(row + col == C - 1, 1.0, 0.0).astype(jnp.bfloat16)
    total = None
    for _ in range(3):
        piece = x.astype(jnp.bfloat16)
        x = x - piece.astype(jnp.float32)
        part = jnp.dot(piece, turn, preferred_element_type=jnp.float32)
        total = part if total is None else total + part
    return total


def kernel(
    p, near_in, flips_in, roots_in, q_in, cour, diff, out,
    q, qt, xs, fields, fpad, coef, meta,
    raw, s2, r2, s3, r3, fraw, fs2, fr2, fs3, fr3,
    send, recv, fsend, frecv, in_sem, out_sem, field_sem, spread_sem, meta_sem, table_sem,
    near, flips, roots,
):
    here = Here(p, 0)
    spec = lax.axis_index("spec")
    sc, nch = p.sc, p.nch

    def plane_in(c, s):
        return pltpu.make_async_copy(
            q_in.at[(c // 2) * sc + s, lax.rem(c, 2)],
            q.at[c, pl.ds(s * PITCH + 8, C), :],
            in_sem.at[c, s],
        )

    def plane_out(c, s):
        return pltpu.make_async_copy(
            q.at[2 * nch + c, pl.ds(s * PITCH + 8, C), :],
            out.at[(c // 2) * sc + s, lax.rem(c, 2)],
            out_sem.at[c, s],
        )

    barrier = pltpu.get_barrier_semaphore()
    partners = [here.at(first=o) for o in range(1, p.a)]
    partners += [here.at(mate=o) for o in range(1, p.m)]
    partners += [here.at(last=o) for o in range(1, p.b)]
    for tile in partners:
        pl.semaphore_signal(barrier, inc=1, device_id={"tile": tile}, device_id_type=MESH)
    for off in range(1, p.members):
        peer = lax.rem(spec + off, p.members)
        pl.semaphore_signal(barrier, inc=1, device_id={"spec": peer}, device_id_type=MESH)

    tables = [
        pltpu.make_async_copy(src, dst, table_sem.at[i])
        for i, (src, dst) in enumerate(((near_in, near), (flips_in, flips), (roots_in, roots)))
    ]
    for copy in tables:
        copy.start()

    @pl.loop(0, nch)
    def _(c):
        for s in range(sc):
            plane_in(c, s).start()

    own_fields = [
        pltpu.make_async_copy(src.at[0], fields.at[t, spec], field_sem.at[t])
        for t, src in enumerate((cour, diff))
    ]
    for copy in own_fields:
        copy.start()
    for copy in tables:
        copy.wait()
    edge_row = lax.broadcasted_iota(jnp.int32, (8, C), 0)
    tile = jnp.full((8, C), near[0, 3], jnp.int32)
    for e in range(3):
        tile = jnp.where(edge_row == e, near[0, e], tile)
    meta[0] = tile

    def spread(t, src, off):
        peer = lax.rem(spec + off, p.members)
        return pltpu.make_async_remote_copy(
            src_ref=src.at[0],
            dst_ref=fields.at[t, spec],
            send_sem=spread_sem.at[0, t, off],
            recv_sem=spread_sem.at[1, t, off],
            device_id={"spec": peer},
            device_id_type=MESH,
        )

    spreads = [
        spread(t, src, off) for off in range(1, p.members) for t, src in enumerate((cour, diff))
    ]
    metas = []
    for way in range(2):
        for o in range(1, p.a):
            i = way * (p.a - 1) + o
            to = here.at(last=o) if way else here.at(first=o)
            metas.append(remote(meta.at[0], meta.at[i], meta_sem.at[0, i], meta_sem.at[1, i], to))

    def data_of(c):
        return Swap(
            p, Here(p, 1 - lax.rem(c, 2)), DATA_EDGES, 24, (raw, s2, r2, s3, r3), (send, recv), meta
        )

    face = Swap(p, here, FACE_EDGES, 8, (fraw, fs2, fr2, fs3, fr3), (fsend, frecv), meta)

    def transpose_planes(src, dst):
        for s in range(sc):
            rows = pl.ds(s * PITCH + 8, C)
            dst[rows, :] = src[rows, :].T

    def pack(u):
        strips = []
        for ref, first in ((qt, 0), (qt, C - 1), (q, 0), (q, C - 1)):
            for d in range(3):
                at = first + d if first == 0 else first - d
                strip = ref[u, pl.ds(8 + at, sc, stride=PITCH), :]
                if sc < 8:
                    strip = jnp.concatenate([strip, jnp.zeros((8 - sc, C), jnp.float32)], 0)
                strips.append(strip)
        turned = reversed_lanes(jnp.concatenate(strips, 0))
        for e in range(4):
            flipped = jnp.full((8, C), flips[0, e], jnp.int32) == 1
            for d in range(3):
                i = 3 * e + d
                raw[u, 0, e, pl.ds(8 * d, 8), :] = jnp.where(
                    flipped, turned[8 * i : 8 * i + 8], strips[i]
                )

    def prepare_fields():
        for copy in own_fields:
            copy.wait()
        for copy in spreads:
            copy.wait_recv()
        for t in range(2):
            for k in range(2):
                root = roots[0, k]
                for lev in range(2):
                    at = ((k * 2 + t) * 2 + lev) * FPITCH
                    fpad[0, pl.ds(at, C), :] = fields[t, root, k, 0, lev].T
                    fpad[1, pl.ds(at, C), :] = fields[t, root, k, 1, lev]

    def pack_faces():
        for i, e in enumerate((0, 2)):
            tile = fpad[i, pl.ds(0, 8, stride=FPITCH), :]
            flipped = jnp.full((8, C), flips[0, e], jnp.int32) == 1
            fraw[0, 0, i] = jnp.where(flipped, reversed_lanes(tile), tile)

    def end_faces():
        for i, tile in enumerate(face.finish(0)):
            fpad[i, pl.ds(C, 8, stride=FPITCH), :] = tile

    def coefficients(k, r):
        at = pl.multiple_of(r * 8, 8)
        for lev in range(2):
            for way in range(2):
                low, high = [], []
                for t in range(2):
                    base = ((k * 2 + t) * 2 + lev) * FPITCH + at
                    low.append(fpad[way, pl.ds(pl.multiple_of(base, 8), 8), :])
                    high.append(fpad[way, pl.ds(base + 1, 8), :])
                values = stencil(taps(*low), taps(*high))
                if way == 1:
                    values[3] = values[3] + 1.0
                for i, value in enumerate(values):
                    coef[k * 2 + lev, way * 7 + i, pl.ds(at, 8), :] = value

    def stencil_rows(k, c, way, src, dst, r):
        at = pl.multiple_of(r * 8, 8)
        which = k * 2 + lax.rem(c, 2)
        w = [coef[which, way * 7 + i, pl.ds(at, 8), :] for i in range(7)]
        for s in range(sc):
            row = s * PITCH + 8 + at
            total = None
            for i, d in enumerate(SHIFTS):
                term = w[i] * src[pl.ds(row + d, 8), :]
                total = term if total is None else total + term
            dst[pl.ds(pl.multiple_of(row, 8), 8), :] = total

    def interior(k, c):
        u = k * nch + c

        @pl.loop(1, C // 8 - 1)
        def _(r):
            stencil_rows(k, c, 0, qt.at[u], xs.at[c], r)

        @pl.loop(1, C // 8 - 1)
        def _(r):
            stencil_rows(k, c, 1, q.at[u], q.at[u + nch], r)

    def complete(k, c):
        u = k * nch + c
        here_q, here_t, next_q = q.at[u], qt.at[u], q.at[u + nch]
        strips = data_of(c).finish(u)
        for e, (ref, low) in enumerate(
            ((here_t, True), (here_t, False), (here_q, True), (here_q, False))
        ):
            for d in range(3):
                at = 7 - d if low else C + 8 + d
                ref[pl.ds(at, sc, stride=PITCH), :] = strips[3 * e + d][:sc]
        for r in (0, C // 8 - 1):
            stencil_rows(k, c, 0, here_t, xs.at[c], r)
            stencil_rows(k, c, 1, here_q, next_q, r)
        for s in range(sc):
            rows = pl.ds(s * PITCH + 8, C)
            next_q[rows, :] = next_q[rows, :] + xs[c, rows, :].T

    def staged(t, delay):
        at = t - delay
        k = at // p.period
        c = at - k * p.period
        return k, c, (at >= 0) & (k < 2) & (c < nch)

    @pl.loop(0, nch)
    def _(c):
        for s in range(sc):
            plane_in(c, s).wait()
        transpose_planes(q.at[c], qt.at[c])
        pack(c)

        @pl.when(c == 0)
        def _():
            pl.semaphore_wait(barrier, len(partners) + p.members - 1)
            for copy in metas + spreads:
                copy.start()

        data_of(c).start(c)

    prepare_fields()
    pack_faces()
    face.start(0)

    @pl.loop(0, C // 8 - 1)
    def _(r):
        coefficients(0, r)
        coefficients(1, r)

    for copy in metas:
        copy.wait_recv()

    @pl.loop(0, p.ticks)
    def _(t):
        k3, c3, on3 = staged(t, p.late)

        @pl.when(on3)
        def _():
            data_of(c3).late(k3 * nch + c3)

        k2, c2, on2 = staged(t, 0)

        @pl.when(on2)
        def _():
            data_of(c2).middle(k2 * nch + c2)

        @pl.when(t == p.face_middle)
        def _():
            face.middle(0)

        @pl.when(t == p.face_late)
        def _():
            face.late(0)

        @pl.when(t < nch)
        def _():
            interior(0, t)

        @pl.when(t == p.end)
        def _():
            end_faces()
            coefficients(0, C // 8 - 1)
            coefficients(1, C // 8 - 1)

        k4, c4, on4 = staged(t, p.end)

        @pl.when(on4)
        def _():
            complete(k4, c4)

            @pl.when(k4 == 0)
            def _():
                transpose_planes(q.at[nch + c4], qt.at[nch + c4])
                pack(nch + c4)
                data_of(c4).start(nch + c4)
                interior(1, c4)

            @pl.when(k4 == 1)
            def _():
                for s in range(sc):
                    plane_out(c4, s).start()

    for copy in metas + spreads:
        copy.wait_send()
    face.drain(0)

    @pl.loop(0, p.nu)
    def _(u):
        data_of(lax.rem(u, nch)).drain(u)

    @pl.loop(0, nch)
    def _(c):
        for s in range(sc):
            plane_out(c, s).wait()


def body(sizes, tracers, courant, diffusivity, edge_blocks, edge_flips, roots):
    p = Plan(sizes, tracers.shape[0])
    anywhere = pl.BlockSpec(memory_space=pl.ANY)
    f32 = jnp.float32
    count = p.a - 1 + 2 * (p.m - 1) + p.b - 1

    def buffers(nu, edges, rows):
        return [
            pltpu.VMEM((nu, p.a, edges, rows, C), f32),
            pltpu.VMEM((nu, p.m - 1, p.a, p.b, rows, C), f32),
            pltpu.VMEM((nu, p.m - 1, p.a, p.b, rows, C), f32),
            pltpu.VMEM((nu, p.b - 1, edges, rows, C), f32),
            pltpu.VMEM((nu, p.b - 1, edges, rows, C), f32),
        ]

    dma = pltpu.SemaphoreType.DMA
    return pl.pallas_call(
        functools.partial(kernel, p),
        out_shape=jax.ShapeDtypeStruct(tracers.shape, tracers.dtype),
        in_specs=[anywhere] * 6,
        out_specs=anywhere,
        scratch_shapes=[
            pltpu.VMEM((3 * p.nch, p.sc * PITCH, C), f32),
            pltpu.VMEM((2 * p.nch, p.sc * PITCH, C), f32),
            pltpu.VMEM((p.nch, p.sc * PITCH, C), f32),
            pltpu.VMEM((2, p.members, 2, 2, 2, C, C), f32),
            pltpu.VMEM((2, 8 * FPITCH, C), f32),
            pltpu.VMEM((4, 14, C, C), f32),
            pltpu.VMEM((p.a + p.b - 1, 8, C), jnp.int32),
            *buffers(p.nu, 4, 24),
            *buffers(1, 2, 8),
            dma((p.nu, count)),
            dma((p.nu, count)),
            dma((1, count)),
            dma((1, count)),
            dma((p.nch, p.sc)),
            dma((p.nch, p.sc)),
            dma((2,)),
            dma((2, 2, p.members)),
            dma((2, p.a + p.b - 1)),
            dma((3,)),
            pltpu.SMEM((1, 4), jnp.int32),
            pltpu.SMEM((1, 4), jnp.int32),
            pltpu.SMEM((1, 2), jnp.int32),
        ],
        compiler_params=pltpu.CompilerParams(
            collective_id=0, has_side_effects=True, vmem_limit_bytes=VMEM_LIMIT
        ),
        name="transport",
    )(edge_blocks, edge_flips, roots.reshape(1, 2), tracers, courant, diffusivity)


def solution(mesh):
    placed = (
        P("spec", None, "tile", None),
        P("spec", None, None, None, "tile", None),
        P("spec", None, None, None, "tile", None),
        P("tile", None),
        P("tile", None),
        P(None, "tile"),
    )
    return jax.shard_map(
        functools.partial(body, dict(mesh.shape)),
        mesh=mesh,
        in_specs=placed,
        out_specs=P("spec", None, "tile", None),
        check_vma=False,
    )
```

```python
import functools

import jax
import jax.numpy as jnp
from jax import lax
from jax.experimental import pallas as pl
from jax.experimental.pallas import tpu as pltpu
from jax.sharding import PartitionSpec as P

MESH = pl.DeviceIdType.MESH
C = 128
PITCH = 144
FPITCH = C + 8
VMEM_LIMIT = 60 * 1024 * 1024
SHIFTS = (-3, -2, -1, 0, 1, 2, 3)
DATA_EDGES = ((0, 1), (1, 0), (2, 3), (3, 2))
FACE_EDGES = ((1, 0), (3, 2))


def taps(c, k):
    s = jnp.abs(c)
    rest = 1.0 - s
    mid = c * rest * rest
    outer = -s * rest
    ahead = (3.0 - 2.0 * s) * s
    pos = jnp.maximum(c, 0.0)
    neg = jnp.minimum(c, 0.0)
    out_pos = pos * outer
    out_neg = neg * outer
    a = 7.0 / 12.0
    b = -1.0 / 12.0
    return [
        b * out_pos,
        b * mid + a * out_pos,
        a * (mid + out_pos) + b * out_neg + pos * ahead + k,
        a * (mid + out_neg) + b * out_pos + neg * ahead - k,
        b * mid + a * out_neg,
        b * out_neg,
    ]


def stencil(low, high):
    lo = low + [None]
    hi = [None] + high
    return [-b if a is None else a if b is None else a - b for a, b in zip(lo, hi)]


class Plan:
    def __init__(self, sizes, species):
        n = sizes["tile"]
        self.members = sizes["spec"]
        self.m = 4
        rest = n // self.m
        self.b = 1
        while self.b * self.b * 4 <= rest:
            self.b *= 2
        self.a = rest // self.b
        self.sc = max(d for d in range(1, 9) if species % d == 0)
        self.nch = 2 * (species // self.sc)
        self.nu = 2 * self.nch
        self.late, self.end, self.turn = 3, 6, 3
        self.face_middle, self.face_late = 1, 3
        self.period = max(self.nch, self.end + self.turn)
        self.ticks = self.period + self.nch + self.end
        assert self.a == self.b and self.a * self.b * self.m == n


class Here:
    def __init__(self, p, swapped):
        self.p, self.swapped = p, swapped
        me = lax.axis_index("tile")
        self.mate = lax.rem(me, p.m)
        low = lax.rem(me // p.m, p.b)
        far = me // (p.m * p.b)
        self.first = far + swapped * (low - far)
        self.last = low + swapped * (far - low)
        self.first_stride = p.m * (p.b + swapped * (1 - p.b))
        self.last_stride = p.m * (1 + swapped * (p.b - 1))

    def at(self, first=0, last=0, mate=0):
        p = self.p
        f = lax.rem(self.first + (first + p.a), p.a)
        w = lax.rem(self.last + (last + p.b), p.b)
        i = lax.rem(self.mate + (mate + p.m), p.m)
        return f * self.first_stride + w * self.last_stride + i

    def near_of_source(self, off):
        return off if off == 0 else off + self.swapped * (self.p.a - 1)

    def near_of_target(self, off):
        return self.p.b - off + (1 - self.swapped) * (self.p.a - 1)


def remote(src, dst, send, recv, tile):
    return pltpu.make_async_remote_copy(
        src_ref=src,
        dst_ref=dst,
        send_sem=send,
        recv_sem=recv,
        device_id={"tile": tile},
        device_id_type=MESH,
    )


class Swap:
    def __init__(self, p, here, edges, rows, bufs, sems, meta):
        self.p, self.here, self.edges, self.rows, self.meta = p, here, edges, rows, meta
        self.raw, self.s2, self.r2, self.s3, self.r3 = bufs
        self.send, self.recv = sems
        p = self.p
        self.at_2a = p.a - 1
        self.at_2b = self.at_2a + p.m - 1
        self.at_3 = self.at_2b + p.m - 1

    def first(self, u, off):
        return remote(
            self.raw.at[u, 0], self.raw.at[u, off], self.send.at[off - 1],
            self.recv.at[u, off - 1], self.here.at(first=off),
        )

    def own_slots(self, u, off):
        i = self.at_2a + off - 1
        return remote(
            self.s2.at[u, off - 1, 0], self.r2.at[u, off - 1, 0], self.send.at[i],
            self.recv.at[u, i], self.here.at(mate=off),
        )

    def far_slots(self, u, off):
        i = self.at_2b + off - 1
        part = pl.ds(1, self.p.a - 1)
        return remote(
            self.s2.at[u, off - 1, part], self.r2.at[u, off - 1, part], self.send.at[i],
            self.recv.at[u, i], self.here.at(mate=off),
        )

    def last(self, u, off):
        i = self.at_3 + off - 1
        return remote(
            self.s3.at[u, off - 1], self.r3.at[u, off - 1], self.send.at[i],
            self.recv.at[u, i], self.here.at(last=off),
        )

    def wanted(self, which, edge):
        return jnp.broadcast_to(self.meta[which, pl.ds(edge, 1), :], (8, C))

    def fill(self, u, source):
        p, here = self.p, self.here
        rows = [self.wanted(here.near_of_source(source), src) for _, src in self.edges]
        index = [j for j in range(len(self.edges))]
        slot_of = {src: j for j, (_, src) in enumerate(sorted(self.edges, key=lambda x: x[1]))}
        for off in range(1, p.m):
            for low in range(p.b):
                dest = here.at(last=low, mate=off)
                masks = [row == dest for row in rows]
                for d in range(self.rows // 8):
                    part = pl.ds(8 * d, 8)
                    value = None
                    for j in index:
                        strip = self.raw[u, source, slot_of[self.edges[j][1]], part, :]
                        value = strip if value is None else jnp.where(masks[j], strip, value)
                    self.s2[u, off - 1, source, low, part, :] = value

    def start(self, u):
        p = self.p
        for off in range(1, p.a):
            self.first(u, off).start()
        self.fill(u, 0)
        for off in range(1, p.m):
            self.own_slots(u, off).start()

    def middle(self, u):
        p = self.p
        for off in range(1, p.a):
            self.first(u, off).wait_recv()
        for off in range(1, p.a):
            self.fill(u, off)
        for off in range(1, p.m):
            self.far_slots(u, off).start()

    def arrived(self, u, low, which):
        p, here = self.p, self.here
        slot_of = {src: j for j, (_, src) in enumerate(sorted(self.edges, key=lambda x: x[1]))}
        result = []
        for j, (dst, src) in enumerate(self.edges):
            want = self.wanted(which, dst)
            sources = []
            for far in range(p.a):
                if low or far:
                    ident = here.at(first=-far)
                    sources.append((want == ident, lambda part, far=far, slot=slot_of[src]: self.raw[u, far, slot, part, :]))
                for off in range(1, p.m):
                    ident = here.at(first=-far, mate=-off)
                    sources.append(
                        (want == ident, lambda part, far=far, off=off: self.r2[u, off - 1, far, low, part, :])
                    )
            result.append((want, sources))
        return result

    def late(self, u):
        p, here = self.p, self.here
        for off in range(1, p.m):
            self.own_slots(u, off).wait_recv()
            self.far_slots(u, off).wait_recv()
        for low in range(1, p.b):
            for j, (_, sources) in enumerate(self.arrived(u, low, here.near_of_target(low))):
                for d in range(self.rows // 8):
                    part = pl.ds(8 * d, 8)
                    value = None
                    for mask, load in sources:
                        value = load(part) if value is None else jnp.where(mask, load(part), value)
                    self.s3[u, low - 1, j, part, :] = value
            self.last(u, low).start()

    def finish(self, u):
        p, here = self.p, self.here
        for off in range(1, p.b):
            self.last(u, off).wait_recv()
        strips = []
        for j, (want, sources) in enumerate(self.arrived(u, 0, 0)):
            for off in range(1, p.b):
                column = self.column(want)
                ident = lax.rem(here.last + (p.b - off), p.b)
                sources.append((column == ident, lambda part, off=off: self.r3[u, off - 1, j, part, :]))
            for d in range(self.rows // 8):
                part = pl.ds(8 * d, 8)
                value = None
                for mask, load in sources:
                    value = load(part) if value is None else jnp.where(mask, load(part), value)
                strips.append(value)
        return strips

    def column(self, want):
        p, here = self.p, self.here
        near, far = lax.rem(lax.div(want, p.m), p.b), lax.div(want, p.m * p.b)
        return near + here.swapped * (far - near)

    def drain(self):
        p = self.p
        sent = [self.raw.at[:, 0]] * (p.a - 1)
        sent += [self.s2.at[:, off - 1, 0] for off in range(1, p.m)]
        sent += [self.s2.at[:, off - 1, pl.ds(1, p.a - 1)] for off in range(1, p.m)]
        sent += [self.s3.at[:, off - 1] for off in range(1, p.b)]
        for i, ref in enumerate(sent):
            pltpu.make_async_copy(ref, ref, self.send.at[i]).wait()


def reversed_lanes(x):
    row = lax.broadcasted_iota(jnp.int32, (C, C), 0)
    col = lax.broadcasted_iota(jnp.int32, (C, C), 1)
    turn = jnp.where(row + col == C - 1, 1.0, 0.0).astype(jnp.bfloat16)
    total = None
    for _ in range(3):
        piece = x.astype(jnp.bfloat16)
        x = x - piece.astype(jnp.float32)
        part = jnp.dot(piece, turn, preferred_element_type=jnp.float32)
        total = part if total is None else total + part
    return total


def kernel(
    p, near_in, flips_in, roots_in, q_in, cour, diff, out,
    q, qt, xs, fields, fpad, coef, meta,
    raw, s2, r2, s3, r3, fraw, fs2, fr2, fs3, fr3,
    send, recv, fsend, frecv, in_sem, field_sem, spread_sem, meta_sem, table_sem,
    near, flips, roots,
):
    here = Here(p, 0)
    spec = lax.axis_index("spec")
    sc, nch = p.sc, p.nch

    def plane_in(c, s):
        return pltpu.make_async_copy(
            q_in.at[(c // 2) * sc + s, lax.rem(c, 2)],
            q.at[c, pl.ds(s * PITCH + 8, C), :],
            in_sem.at[c],
        )

    barrier = pltpu.get_barrier_semaphore()
    partners = [here.at(first=o) for o in range(1, p.a)]
    partners += [here.at(mate=o) for o in range(1, p.m)]
    partners += [here.at(last=o) for o in range(1, p.b)]
    for tile in partners:
        pl.semaphore_signal(barrier, inc=1, device_id={"tile": tile}, device_id_type=MESH)
    for off in range(1, p.members):
        peer = lax.rem(spec + off, p.members)
        pl.semaphore_signal(barrier, inc=1, device_id={"spec": peer}, device_id_type=MESH)

    tables = [
        pltpu.make_async_copy(src, dst, table_sem.at[i])
        for i, (src, dst) in enumerate(((near_in, near), (flips_in, flips), (roots_in, roots)))
    ]
    for copy in tables:
        copy.start()

    def planes_in(c):
        for s in range(sc):
            plane_in(c, s).start()

    planes_in(0)
    own_fields = [
        pltpu.make_async_copy(src.at[0], fields.at[t, spec], field_sem.at[t])
        for t, src in enumerate((cour, diff))
    ]
    for copy in tables:
        copy.wait()
    edge_row = lax.broadcasted_iota(jnp.int32, (8, C), 0)
    tile = jnp.full((8, C), near[0, 3], jnp.int32)
    for e in range(3):
        tile = jnp.where(edge_row == e, near[0, e], tile)
    meta[0] = tile

    def spread(t, src, off):
        peer = lax.rem(spec + off, p.members)
        return pltpu.make_async_remote_copy(
            src_ref=src.at[0],
            dst_ref=fields.at[t, spec],
            send_sem=spread_sem.at[0, t, off],
            recv_sem=spread_sem.at[1, t, off],
            device_id={"spec": peer},
            device_id_type=MESH,
        )

    spreads = [
        spread(t, src, off) for off in range(1, p.members) for t, src in enumerate((cour, diff))
    ]
    metas = []
    for way in range(2):
        for o in range(1, p.a):
            i = way * (p.a - 1) + o
            to = here.at(last=o) if way else here.at(first=o)
            metas.append(remote(meta.at[0], meta.at[i], meta_sem.at[0, i], meta_sem.at[1, i], to))

    def data_of(c):
        return Swap(
            p, Here(p, 1 - lax.rem(c, 2)), DATA_EDGES, 24, (raw, s2, r2, s3, r3), (send, recv), meta
        )

    face = Swap(p, here, FACE_EDGES, 8, (fraw, fs2, fr2, fs3, fr3), (fsend, frecv), meta)

    def transpose_planes(src, dst):
        for s in range(sc):
            rows = pl.ds(s * PITCH + 8, C)
            dst[rows, :] = src[rows, :].T

    def pack(u):
        strips = []
        for ref, first in ((qt, 0), (qt, C - 1), (q, 0), (q, C - 1)):
            for d in range(3):
                at = first + d if first == 0 else first - d
                strip = ref[u, pl.ds(8 + at, sc, stride=PITCH), :]
                if sc < 8:
                    strip = jnp.concatenate([strip, jnp.zeros((8 - sc, C), jnp.float32)], 0)
                strips.append(strip)
        turned = reversed_lanes(jnp.concatenate(strips, 0))
        for e in range(4):
            flipped = jnp.full((8, C), flips[0, e], jnp.int32) == 1
            for d in range(3):
                i = 3 * e + d
                raw[u, 0, e, pl.ds(8 * d, 8), :] = jnp.where(
                    flipped, turned[8 * i : 8 * i + 8], strips[i]
                )

    def prepare_fields():
        for copy in own_fields:
            copy.wait()
        for copy in spreads:
            copy.wait_recv()
        for t in range(2):
            for k in range(2):
                root = roots[0, k]
                for lev in range(2):
                    at = ((k * 2 + t) * 2 + lev) * FPITCH
                    fpad[0, pl.ds(at, C), :] = fields[t, root, k, 0, lev].T
                    fpad[1, pl.ds(at, C), :] = fields[t, root, k, 1, lev]

    def pack_faces():
        for i, e in enumerate((0, 2)):
            tile = fpad[i, pl.ds(0, 8, stride=FPITCH), :]
            flipped = jnp.full((8, C), flips[0, e], jnp.int32) == 1
            fraw[0, 0, i] = jnp.where(flipped, reversed_lanes(tile), tile)

    def end_faces():
        for i, tile in enumerate(face.finish(0)):
            fpad[i, pl.ds(C, 8, stride=FPITCH), :] = tile

    def coefficients(k, r):
        at = pl.multiple_of(r * 8, 8)
        for lev in range(2):
            for way in range(2):
                low, high = [], []
                for t in range(2):
                    base = ((k * 2 + t) * 2 + lev) * FPITCH + at
                    low.append(fpad[way, pl.ds(pl.multiple_of(base, 8), 8), :])
                    high.append(fpad[way, pl.ds(base + 1, 8), :])
                values = stencil(taps(*low), taps(*high))
                if way == 1:
                    values[3] = values[3] + 1.0
                for i, value in enumerate(values):
                    coef[k * 2 + lev, way * 7 + i, pl.ds(at, 8), :] = value

    def stencil_rows(k, c, way, src, dst, r):
        at = pl.multiple_of(r * 8, 8)
        which = k * 2 + lax.rem(c, 2)
        w = [coef[which, way * 7 + i, pl.ds(at, 8), :] for i in range(7)]
        for s in range(sc):
            row = s * PITCH + 8 + at
            total = None
            for i, d in enumerate(SHIFTS):
                term = w[i] * src[pl.ds(row + d, 8), :]
                total = term if total is None else total + term
            dst[pl.ds(pl.multiple_of(row, 8), 8), :] = total

    def interior(k, c):
        u = k * nch + c

        @pl.loop(1, C // 8 - 1)
        def _(r):
            stencil_rows(k, c, 0, qt.at[u], xs.at[c], r)

        @pl.loop(1, C // 8 - 1)
        def _(r):
            stencil_rows(k, c, 1, q.at[u], q.at[u + nch], r)

    def complete(k, c):
        u = k * nch + c
        here_q, here_t, next_q = q.at[u], qt.at[u], q.at[u + nch]
        strips = data_of(c).finish(u)
        for e, (ref, low) in enumerate(
            ((here_t, True), (here_t, False), (here_q, True), (here_q, False))
        ):
            for d in range(3):
                at = 7 - d if low else C + 8 + d
                ref[pl.ds(at, sc, stride=PITCH), :] = strips[3 * e + d][:sc]
        for r in (0, C // 8 - 1):
            stencil_rows(k, c, 0, here_t, xs.at[c], r)
            stencil_rows(k, c, 1, here_q, next_q, r)

    def joined(k, c, s):
        rows = pl.ds(s * PITCH + 8, C)
        return q[(k + 1) * nch + c, rows, :] + xs[c, rows, :].T

    def staged(t, delay):
        at = t - delay
        k = at // p.period
        c = at - k * p.period
        return k, c, (at >= 0) & (k < 2) & (c < nch)

    @pl.loop(0, nch)
    def _(c):
        @pl.when(c + 1 < nch)
        def _():
            planes_in(c + 1)

        landed = q.at[c, pl.ds(0, sc * C), :]
        pltpu.make_async_copy(landed, landed, in_sem.at[c]).wait()
        transpose_planes(q.at[c], qt.at[c])
        pack(c)

        @pl.when(c == 0)
        def _():
            pl.semaphore_wait(barrier, len(partners) + p.members - 1)

        data_of(c).start(c)

        @pl.when(c == 0)
        def _():
            for copy in metas + spreads + own_fields:
                copy.start()

    prepare_fields()
    pack_faces()
    face.start(0)

    @pl.loop(0, C // 8 - 1)
    def _(r):
        coefficients(0, r)
        coefficients(1, r)

    for copy in metas:
        copy.wait_recv()

    def do_late(t):
        k, c, on = staged(t, p.late)

        @pl.when(on)
        def _():
            data_of(c).late(k * nch + c)

        @pl.when(t == p.face_late)
        def _():
            face.late(0)

    def do_middle(t):
        k, c, on = staged(t, 0)

        @pl.when(on)
        def _():
            data_of(c).middle(k * nch + c)

        @pl.when(t == p.face_middle)
        def _():
            face.middle(0)

    def do_interior(t):
        @pl.when(t < nch)
        def _():
            interior(0, t)

    def do_end(t):
        @pl.when(t == p.end)
        def _():
            end_faces()
            coefficients(0, C // 8 - 1)
            coefficients(1, C // 8 - 1)

        k, c, on = staged(t, p.end)

        @pl.when(on)
        def _():
            complete(k, c)

            @pl.when(k == 0)
            def _():
                for s in range(sc):
                    rows = pl.ds(s * PITCH + 8, C)
                    plane = joined(0, c, s)
                    q[nch + c, rows, :] = plane
                    qt[nch + c, rows, :] = plane.T
                pack(nch + c)
                data_of(c).start(nch + c)
                interior(1, c)

            @pl.when(k == 1)
            def _():
                for s in range(sc):
                    out[(c // 2) * sc + s, lax.rem(c, 2)] = joined(1, c, s)

    @pl.loop(0, p.ticks)
    def _(t):
        for part in (do_middle, do_late, do_interior, do_end):
            part(t)

    for copy in metas + spreads:
        copy.wait_send()
    face.drain()
    data_of(0).drain()


def body(sizes, tracers, courant, diffusivity, edge_blocks, edge_flips, roots):
    p = Plan(sizes, tracers.shape[0])
    anywhere = pl.BlockSpec(memory_space=pl.ANY)
    f32 = jnp.float32
    count = p.a - 1 + 2 * (p.m - 1) + p.b - 1

    def buffers(nu, edges, rows):
        return [
            pltpu.VMEM((nu, p.a, edges, rows, C), f32),
            pltpu.VMEM((nu, p.m - 1, p.a, p.b, rows, C), f32),
            pltpu.VMEM((nu, p.m - 1, p.a, p.b, rows, C), f32),
            pltpu.VMEM((nu, p.b - 1, edges, rows, C), f32),
            pltpu.VMEM((nu, p.b - 1, edges, rows, C), f32),
        ]

    dma = pltpu.SemaphoreType.DMA
    return pl.pallas_call(
        functools.partial(kernel, p),
        out_shape=pltpu.VMEM(tracers.shape, tracers.dtype),
        in_specs=[anywhere] * 6,
        out_specs=pl.BlockSpec(memory_space=pltpu.VMEM),
        scratch_shapes=[
            pltpu.VMEM((3 * p.nch, p.sc * PITCH, C), f32),
            pltpu.VMEM((2 * p.nch, p.sc * PITCH, C), f32),
            pltpu.VMEM((p.nch, p.sc * PITCH, C), f32),
            pltpu.VMEM((2, p.members, 2, 2, 2, C, C), f32),
            pltpu.VMEM((2, 8 * FPITCH, C), f32),
            pltpu.VMEM((4, 14, C, C), f32),
            pltpu.VMEM((p.a + p.b - 1, 8, C), jnp.int32),
            *buffers(p.nu, 4, 24),
            *buffers(1, 2, 8),
            dma((count,)),
            dma((p.nu, count)),
            dma((count,)),
            dma((1, count)),
            dma((p.nch,)),
            dma((2,)),
            dma((2, 2, p.members)),
            dma((2, p.a + p.b - 1)),
            dma((3,)),
            pltpu.SMEM((1, 4), jnp.int32),
            pltpu.SMEM((1, 4), jnp.int32),
            pltpu.SMEM((1, 2), jnp.int32),
        ],
        compiler_params=pltpu.CompilerParams(
            collective_id=0, has_side_effects=True, vmem_limit_bytes=VMEM_LIMIT
        ),
        name="transport",
    )(edge_blocks, edge_flips, roots.reshape(1, 2), tracers, courant, diffusivity)


def solution(mesh):
    placed = (
        P("spec", None, "tile", None),
        P("spec", None, None, None, "tile", None),
        P("spec", None, None, None, "tile", None),
        P("tile", None),
        P("tile", None),
        P(None, "tile"),
    )
    return jax.shard_map(
        functools.partial(body, dict(mesh.shape)),
        mesh=mesh,
        in_specs=placed,
        out_specs=P("spec", None, "tile", None),
        check_vma=False,
    )
```

```python
import functools

import jax
import jax.numpy as jnp
from jax import lax
from jax.experimental import pallas as pl
from jax.experimental.pallas import tpu as pltpu
from jax.sharding import PartitionSpec as P

MESH = pl.DeviceIdType.MESH
C = 128
PITCH = 144
FPITCH = C + 8
VMEM_LIMIT = 60 * 1024 * 1024
SHIFTS = (-3, -2, -1, 0, 1, 2, 3)
DATA_EDGES = ((0, 1), (1, 0), (2, 3), (3, 2))
FACE_EDGES = ((1, 0), (3, 2))


def taps(c, k):
    s = jnp.abs(c)
    rest = 1.0 - s
    mid = c * rest * rest
    outer = -s * rest
    ahead = (3.0 - 2.0 * s) * s
    pos = jnp.maximum(c, 0.0)
    neg = jnp.minimum(c, 0.0)
    out_pos = pos * outer
    out_neg = neg * outer
    a = 7.0 / 12.0
    b = -1.0 / 12.0
    return [
        b * out_pos,
        b * mid + a * out_pos,
        a * (mid + out_pos) + b * out_neg + pos * ahead + k,
        a * (mid + out_neg) + b * out_pos + neg * ahead - k,
        b * mid + a * out_neg,
        b * out_neg,
    ]


def stencil(low, high):
    lo = low + [None]
    hi = [None] + high
    return [-b if a is None else a if b is None else a - b for a, b in zip(lo, hi)]


class Plan:
    def __init__(self, sizes, species):
        n = sizes["tile"]
        self.members = sizes["spec"]
        self.m = 4
        rest = n // self.m
        self.b = 1
        while self.b * self.b * 4 <= rest:
            self.b *= 2
        self.a = rest // self.b
        self.sc = max(d for d in range(1, 9) if species % d == 0)
        self.nch = 2 * (species // self.sc)
        self.nu = 2 * self.nch
        self.late, self.end, self.turn = 3, 6, 3
        self.face_middle, self.face_late = 1, 3
        self.period = max(self.nch, self.end + self.turn)
        self.ticks = self.period + self.nch + self.end
        assert self.a == self.b and self.a * self.b * self.m == n


class Here:
    def __init__(self, p, swapped):
        self.p, self.swapped = p, swapped
        me = lax.axis_index("tile")
        self.mate = lax.rem(me, p.m)
        low = lax.rem(me // p.m, p.b)
        far = me // (p.m * p.b)
        self.first = far + swapped * (low - far)
        self.last = low + swapped * (far - low)
        self.first_stride = p.m * (p.b + swapped * (1 - p.b))
        self.last_stride = p.m * (1 + swapped * (p.b - 1))

    def at(self, first=0, last=0, mate=0):
        p = self.p
        f = lax.rem(self.first + (first + p.a), p.a)
        w = lax.rem(self.last + (last + p.b), p.b)
        i = lax.rem(self.mate + (mate + p.m), p.m)
        return f * self.first_stride + w * self.last_stride + i

    def near_of_source(self, off):
        return off if off == 0 else off + self.swapped * (self.p.a - 1)

    def near_of_target(self, off):
        return self.p.b - off + (1 - self.swapped) * (self.p.a - 1)


def remote(src, dst, send, recv, tile):
    return pltpu.make_async_remote_copy(
        src_ref=src,
        dst_ref=dst,
        send_sem=send,
        recv_sem=recv,
        device_id={"tile": tile},
        device_id_type=MESH,
    )


def landed(ref, sem):
    pltpu.make_async_copy(ref, ref, sem).wait()


class Swap:
    def __init__(self, p, here, edges, rows, bufs, sems, meta):
        self.p, self.here, self.edges, self.rows, self.meta = p, here, edges, rows, meta
        self.raw, self.s2, self.r2, self.s3, self.r3 = bufs
        self.send, self.recv = sems
        p = self.p

    def first(self, u, off):
        return remote(
            self.raw.at[u, 0], self.raw.at[u, off], self.send.at[0, off],
            self.recv.at[u, 0], self.here.at(first=off),
        )

    def own_slots(self, u, off):
        return remote(
            self.s2.at[u, off - 1, 0], self.r2.at[u, off - 1, 0], self.send.at[1, 0],
            self.recv.at[u, 1], self.here.at(mate=off),
        )

    def far_slots(self, u, off):
        part = pl.ds(1, self.p.a - 1)
        return remote(
            self.s2.at[u, off - 1, part], self.r2.at[u, off - 1, part], self.send.at[1, 0],
            self.recv.at[u, 1], self.here.at(mate=off),
        )

    def last(self, u, off):
        return remote(
            self.s3.at[u, off - 1], self.r3.at[u, off - 1], self.send.at[2, 0],
            self.recv.at[u, 2], self.here.at(last=off),
        )

    def wanted(self, which, edge):
        return jnp.broadcast_to(self.meta[which, pl.ds(edge, 1), :], (8, C))

    def fill(self, u, source):
        p, here = self.p, self.here
        rows = [self.wanted(here.near_of_source(source), src) for _, src in self.edges]
        index = [j for j in range(len(self.edges))]
        slot_of = {src: j for j, (_, src) in enumerate(sorted(self.edges, key=lambda x: x[1]))}
        for off in range(1, p.m):
            for low in range(p.b):
                dest = here.at(last=low, mate=off)
                masks = [row == dest for row in rows]
                for d in range(self.rows // 8):
                    part = pl.ds(8 * d, 8)
                    value = None
                    for j in index:
                        strip = self.raw[u, source, slot_of[self.edges[j][1]], part, :]
                        value = strip if value is None else jnp.where(masks[j], strip, value)
                    self.s2[u, off - 1, source, low, part, :] = value

    def start(self, u):
        p = self.p
        for off in range(1, p.a):
            self.first(u, off).start()
        self.fill(u, 0)
        for off in range(1, p.m):
            self.own_slots(u, off).start()

    def middle(self, u):
        p = self.p
        landed(self.raw.at[u, pl.ds(1, p.a - 1)], self.recv.at[u, 0])
        for off in range(1, p.a):
            self.fill(u, off)
        for off in range(1, p.m):
            self.far_slots(u, off).start()

    def arrived(self, u, low, which):
        p, here = self.p, self.here
        slot_of = {src: j for j, (_, src) in enumerate(sorted(self.edges, key=lambda x: x[1]))}
        result = []
        for j, (dst, src) in enumerate(self.edges):
            want = self.wanted(which, dst)
            sources = []
            for far in range(p.a):
                if low or far:
                    ident = here.at(first=-far)
                    sources.append((want == ident, lambda part, far=far, slot=slot_of[src]: self.raw[u, far, slot, part, :]))
                for off in range(1, p.m):
                    ident = here.at(first=-far, mate=-off)
                    sources.append(
                        (want == ident, lambda part, far=far, off=off: self.r2[u, off - 1, far, low, part, :])
                    )
            result.append((want, sources))
        return result

    def late(self, u):
        p, here = self.p, self.here
        landed(self.r2.at[u], self.recv.at[u, 1])
        for low in range(1, p.b):
            for j, (_, sources) in enumerate(self.arrived(u, low, here.near_of_target(low))):
                for d in range(self.rows // 8):
                    part = pl.ds(8 * d, 8)
                    value = None
                    for mask, load in sources:
                        value = load(part) if value is None else jnp.where(mask, load(part), value)
                    self.s3[u, low - 1, j, part, :] = value
            self.last(u, low).start()

    def finish(self, u):
        p, here = self.p, self.here
        landed(self.r3.at[u], self.recv.at[u, 2])
        strips = []
        for j, (want, sources) in enumerate(self.arrived(u, 0, 0)):
            for off in range(1, p.b):
                column = self.column(want)
                ident = lax.rem(here.last + (p.b - off), p.b)
                sources.append((column == ident, lambda part, off=off: self.r3[u, off - 1, j, part, :]))
            for d in range(self.rows // 8):
                part = pl.ds(8 * d, 8)
                value = None
                for mask, load in sources:
                    value = load(part) if value is None else jnp.where(mask, load(part), value)
                strips.append(value)
        return strips

    def column(self, want):
        p, here = self.p, self.here
        near, far = lax.rem(lax.div(want, p.m), p.b), lax.div(want, p.m * p.b)
        return near + here.swapped * (far - near)

    def drain(self):
        p = self.p
        for off in range(1, p.a):
            landed(self.raw.at[:, 0], self.send.at[0, off])
        landed(self.s2, self.send.at[1, 0])
        landed(self.s3, self.send.at[2, 0])


def reversed_lanes(x):
    row = lax.broadcasted_iota(jnp.int32, (C, C), 0)
    col = lax.broadcasted_iota(jnp.int32, (C, C), 1)
    turn = jnp.where(row + col == C - 1, 1.0, 0.0).astype(jnp.bfloat16)
    total = None
    for _ in range(3):
        piece = x.astype(jnp.bfloat16)
        x = x - piece.astype(jnp.float32)
        part = jnp.dot(piece, turn, preferred_element_type=jnp.float32)
        total = part if total is None else total + part
    return total


def kernel(
    p, near_in, flips_in, roots_in, q_in, cour, diff, out,
    q, qt, xs, fields, fpad, coef, meta,
    raw, s2, r2, s3, r3, fraw, fs2, fr2, fs3, fr3,
    send, recv, fsend, frecv, in_sem, field_sem, spread_sem, meta_sem, table_sem,
    near, flips, roots,
):
    here = Here(p, 0)
    spec = lax.axis_index("spec")
    sc, nch = p.sc, p.nch

    def plane_in(c, s):
        return pltpu.make_async_copy(
            q_in.at[(c // 2) * sc + s, lax.rem(c, 2)],
            q.at[c, pl.ds(s * PITCH + 8, C), :],
            in_sem.at[c],
        )

    barrier = pltpu.get_barrier_semaphore()
    partners = [here.at(first=o) for o in range(1, p.a)]
    partners += [here.at(mate=o) for o in range(1, p.m)]
    partners += [here.at(last=o) for o in range(1, p.b)]
    for tile in partners:
        pl.semaphore_signal(barrier, inc=1, device_id={"tile": tile}, device_id_type=MESH)
    for off in range(1, p.members):
        peer = lax.rem(spec + off, p.members)
        pl.semaphore_signal(barrier, inc=1, device_id={"spec": peer}, device_id_type=MESH)

    tables = [
        pltpu.make_async_copy(src, dst, table_sem.at[i])
        for i, (src, dst) in enumerate(((near_in, near), (flips_in, flips), (roots_in, roots)))
    ]
    for copy in tables:
        copy.start()

    def planes_in(c):
        for s in range(sc):
            plane_in(c, s).start()

    planes_in(0)
    own_fields = [
        pltpu.make_async_copy(src.at[0], fields.at[t, spec], field_sem.at[t])
        for t, src in enumerate((cour, diff))
    ]
    for copy in tables:
        copy.wait()
    edge_row = lax.broadcasted_iota(jnp.int32, (8, C), 0)
    tile = jnp.full((8, C), near[0, 3], jnp.int32)
    for e in range(3):
        tile = jnp.where(edge_row == e, near[0, e], tile)
    meta[0] = tile

    def spread(t, src, off):
        peer = lax.rem(spec + off, p.members)
        return pltpu.make_async_remote_copy(
            src_ref=src.at[0],
            dst_ref=fields.at[t, spec],
            send_sem=spread_sem.at[0, t, off - 1],
            recv_sem=spread_sem.at[1, t, off - 1],
            device_id={"spec": peer},
            device_id_type=MESH,
        )

    spreads = [
        spread(t, src, off) for off in range(1, p.members) for t, src in enumerate((cour, diff))
    ]
    metas = []
    for way in range(2):
        for o in range(1, p.a):
            i = way * (p.a - 1) + o
            to = here.at(last=o) if way else here.at(first=o)
            metas.append(remote(meta.at[0], meta.at[i], meta_sem.at[0, i - 1], meta_sem.at[1, i - 1], to))

    def data_of(c):
        return Swap(
            p, Here(p, 1 - lax.rem(c, 2)), DATA_EDGES, 24, (raw, s2, r2, s3, r3), (send, recv), meta
        )

    face = Swap(p, here, FACE_EDGES, 8, (fraw, fs2, fr2, fs3, fr3), (fsend, frecv), meta)

    def transpose_planes(src, dst):
        for s in range(sc):
            rows = pl.ds(s * PITCH + 8, C)
            dst[rows, :] = src[rows, :].T

    def pack(u):
        strips = []
        for ref, first in ((qt, 0), (qt, C - 1), (q, 0), (q, C - 1)):
            for d in range(3):
                at = first + d if first == 0 else first - d
                strip = ref[u, pl.ds(8 + at, sc, stride=PITCH), :]
                if sc < 8:
                    strip = jnp.concatenate([strip, jnp.zeros((8 - sc, C), jnp.float32)], 0)
                strips.append(strip)
        turned = reversed_lanes(jnp.concatenate(strips, 0))
        for e in range(4):
            flipped = jnp.full((8, C), flips[0, e], jnp.int32) == 1
            for d in range(3):
                i = 3 * e + d
                raw[u, 0, e, pl.ds(8 * d, 8), :] = jnp.where(
                    flipped, turned[8 * i : 8 * i + 8], strips[i]
                )

    def prepare_fields():
        for copy in own_fields:
            copy.wait()
        for copy in spreads:
            copy.wait_recv()
        for t in range(2):
            for k in range(2):
                root = roots[0, k]
                for lev in range(2):
                    at = ((k * 2 + t) * 2 + lev) * FPITCH
                    fpad[0, pl.ds(at, C), :] = fields[t, root, k, 0, lev].T
                    fpad[1, pl.ds(at, C), :] = fields[t, root, k, 1, lev]

    def pack_faces():
        for i, e in enumerate((0, 2)):
            tile = fpad[i, pl.ds(0, 8, stride=FPITCH), :]
            flipped = jnp.full((8, C), flips[0, e], jnp.int32) == 1
            fraw[0, 0, i] = jnp.where(flipped, reversed_lanes(tile), tile)

    def end_faces():
        for i, tile in enumerate(face.finish(0)):
            fpad[i, pl.ds(C, 8, stride=FPITCH), :] = tile

    def coefficients(k, r):
        at = pl.multiple_of(r * 8, 8)
        for lev in range(2):
            for way in range(2):
                low, high = [], []
                for t in range(2):
                    base = ((k * 2 + t) * 2 + lev) * FPITCH + at
                    low.append(fpad[way, pl.ds(pl.multiple_of(base, 8), 8), :])
                    high.append(fpad[way, pl.ds(base + 1, 8), :])
                values = stencil(taps(*low), taps(*high))
                if way == 1:
                    values[3] = values[3] + 1.0
                for i, value in enumerate(values):
                    coef[k * 2 + lev, way * 7 + i, pl.ds(at, 8), :] = value

    def stencil_rows(k, c, way, src, dst, r):
        at = pl.multiple_of(r * 8, 8)
        which = k * 2 + lax.rem(c, 2)
        w = [coef[which, way * 7 + i, pl.ds(at, 8), :] for i in range(7)]
        for s in range(sc):
            row = s * PITCH + 8 + at
            total = None
            for i, d in enumerate(SHIFTS):
                term = w[i] * src[pl.ds(row + d, 8), :]
                total = term if total is None else total + term
            dst[pl.ds(pl.multiple_of(row, 8), 8), :] = total

    def interior(k, c):
        u = k * nch + c

        @pl.loop(1, C // 8 - 1)
        def _(r):
            stencil_rows(k, c, 0, qt.at[u], xs.at[c], r)

        @pl.loop(1, C // 8 - 1)
        def _(r):
            stencil_rows(k, c, 1, q.at[u], q.at[u + nch], r)

    def complete(k, c):
        u = k * nch + c
        here_q, here_t, next_q = q.at[u], qt.at[u], q.at[u + nch]
        strips = data_of(c).finish(u)
        for e, (ref, low) in enumerate(
            ((here_t, True), (here_t, False), (here_q, True), (here_q, False))
        ):
            for d in range(3):
                at = 7 - d if low else C + 8 + d
                ref[pl.ds(at, sc, stride=PITCH), :] = strips[3 * e + d][:sc]
        for r in (0, C // 8 - 1):
            stencil_rows(k, c, 0, here_t, xs.at[c], r)
            stencil_rows(k, c, 1, here_q, next_q, r)

    def joined(k, c, s):
        rows = pl.ds(s * PITCH + 8, C)
        return q[(k + 1) * nch + c, rows, :] + xs[c, rows, :].T

    def staged(t, delay):
        at = t - delay
        k = at // p.period
        c = at - k * p.period
        return k, c, (at >= 0) & (k < 2) & (c < nch)

    @pl.loop(0, nch)
    def _(c):
        @pl.when(c + 1 < nch)
        def _():
            planes_in(c + 1)

        landed(q.at[c, pl.ds(0, sc * C), :], in_sem.at[c])
        transpose_planes(q.at[c], qt.at[c])
        pack(c)

        @pl.when(c == 0)
        def _():
            pl.semaphore_wait(barrier, len(partners) + p.members - 1)

        data_of(c).start(c)

        @pl.when(c == 0)
        def _():
            for copy in metas + spreads + own_fields:
                copy.start()

    prepare_fields()
    pack_faces()
    face.start(0)

    @pl.loop(0, C // 8 - 1)
    def _(r):
        coefficients(0, r)
        coefficients(1, r)

    for copy in metas:
        copy.wait_recv()

    def do_late(t):
        k, c, on = staged(t, p.late)

        @pl.when(on)
        def _():
            data_of(c).late(k * nch + c)

        @pl.when(t == p.face_late)
        def _():
            face.late(0)

    def do_middle(t):
        k, c, on = staged(t, 0)

        @pl.when(on)
        def _():
            data_of(c).middle(k * nch + c)

        @pl.when(t == p.face_middle)
        def _():
            face.middle(0)

    def do_interior(t):
        @pl.when(t < nch)
        def _():
            interior(0, t)

    def do_end(t):
        @pl.when(t == p.end)
        def _():
            end_faces()
            coefficients(0, C // 8 - 1)
            coefficients(1, C // 8 - 1)

        k, c, on = staged(t, p.end)

        @pl.when(on)
        def _():
            complete(k, c)

            @pl.when(k == 0)
            def _():
                for s in range(sc):
                    rows = pl.ds(s * PITCH + 8, C)
                    plane = joined(0, c, s)
                    q[nch + c, rows, :] = plane
                    qt[nch + c, rows, :] = plane.T
                pack(nch + c)
                data_of(c).start(nch + c)
                interior(1, c)

            @pl.when(k == 1)
            def _():
                for s in range(sc):
                    out[(c // 2) * sc + s, lax.rem(c, 2)] = joined(1, c, s)

    @pl.loop(0, p.ticks)
    def _(t):
        for part in (do_middle, do_late, do_interior, do_end):
            part(t)

    for copy in metas + spreads:
        copy.wait_send()
    face.drain()
    data_of(0).drain()


def body(sizes, tracers, courant, diffusivity, edge_blocks, edge_flips, roots):
    p = Plan(sizes, tracers.shape[0])
    anywhere = pl.BlockSpec(memory_space=pl.ANY)
    f32 = jnp.float32

    def buffers(nu, edges, rows):
        return [
            pltpu.VMEM((nu, p.a, edges, rows, C), f32),
            pltpu.VMEM((nu, p.m - 1, p.a, p.b, rows, C), f32),
            pltpu.VMEM((nu, p.m - 1, p.a, p.b, rows, C), f32),
            pltpu.VMEM((nu, p.b - 1, edges, rows, C), f32),
            pltpu.VMEM((nu, p.b - 1, edges, rows, C), f32),
        ]

    dma = pltpu.SemaphoreType.DMA
    return pl.pallas_call(
        functools.partial(kernel, p),
        out_shape=pltpu.VMEM(tracers.shape, tracers.dtype),
        in_specs=[anywhere] * 6,
        out_specs=pl.BlockSpec(memory_space=pltpu.VMEM),
        scratch_shapes=[
            pltpu.VMEM((3 * p.nch, p.sc * PITCH, C), f32),
            pltpu.VMEM((2 * p.nch, p.sc * PITCH, C), f32),
            pltpu.VMEM((p.nch, p.sc * PITCH, C), f32),
            pltpu.VMEM((2, p.members, 2, 2, 2, C, C), f32),
            pltpu.VMEM((2, 8 * FPITCH, C), f32),
            pltpu.VMEM((4, 14, C, C), f32),
            pltpu.VMEM((p.a + p.b - 1, 8, C), jnp.int32),
            *buffers(p.nu, 4, 24),
            *buffers(1, 2, 8),
            dma((3, p.a)),
            dma((p.nu, 3)),
            dma((3, p.a)),
            dma((1, 3)),
            dma((p.nch,)),
            dma((2,)),
            dma((2, 2, p.members - 1)),
            dma((2, p.a + p.b - 2)),
            dma((3,)),
            pltpu.SMEM((1, 4), jnp.int32),
            pltpu.SMEM((1, 4), jnp.int32),
            pltpu.SMEM((1, 2), jnp.int32),
        ],
        compiler_params=pltpu.CompilerParams(
            collective_id=0, has_side_effects=True, vmem_limit_bytes=VMEM_LIMIT
        ),
        name="transport",
    )(edge_blocks, edge_flips, roots.reshape(1, 2), tracers, courant, diffusivity)


def solution(mesh):
    placed = (
        P("spec", None, "tile", None),
        P("spec", None, None, None, "tile", None),
        P("spec", None, None, None, "tile", None),
        P("tile", None),
        P("tile", None),
        P(None, "tile"),
    )
    return jax.shard_map(
        functools.partial(body, dict(mesh.shape)),
        mesh=mesh,
        in_specs=placed,
        out_specs=P("spec", None, "tile", None),
        check_vma=False,
    )
```

```python
import functools

import jax
import jax.numpy as jnp
from jax import lax
from jax.experimental import pallas as pl
from jax.experimental.pallas import tpu as pltpu
from jax.sharding import PartitionSpec as P

MESH = pl.DeviceIdType.MESH
C = 128
PITCH = 144
FPITCH = C + 8
VMEM_LIMIT = 60 * 1024 * 1024
SHIFTS = (-3, -2, -1, 0, 1, 2, 3)
DATA_EDGES = ((0, 1), (1, 0), (2, 3), (3, 2))
FACE_EDGES = ((1, 0), (3, 2))


def taps(c, k):
    s = jnp.abs(c)
    rest = 1.0 - s
    mid = c * rest * rest
    outer = -s * rest
    ahead = (3.0 - 2.0 * s) * s
    pos = jnp.maximum(c, 0.0)
    neg = jnp.minimum(c, 0.0)
    out_pos = pos * outer
    out_neg = neg * outer
    a = 7.0 / 12.0
    b = -1.0 / 12.0
    return [
        b * out_pos,
        b * mid + a * out_pos,
        a * (mid + out_pos) + b * out_neg + pos * ahead + k,
        a * (mid + out_neg) + b * out_pos + neg * ahead - k,
        b * mid + a * out_neg,
        b * out_neg,
    ]


def stencil(low, high):
    lo = low + [None]
    hi = [None] + high
    return [-b if a is None else a if b is None else a - b for a, b in zip(lo, hi)]


class Plan:
    def __init__(self, sizes, species):
        n = sizes["tile"]
        self.members = sizes["spec"]
        self.m = 4
        rest = n // self.m
        self.b = 1
        while self.b * self.b * 4 <= rest:
            self.b *= 2
        self.a = rest // self.b
        self.sc = max(d for d in range(1, 9) if species % d == 0)
        self.nch = 2 * (species // self.sc)
        self.nu = 2 * self.nch
        self.late, self.end, self.turn = 3, 6, 3
        self.face_middle, self.face_late = 1, 3
        self.period = max(self.nch, self.end + self.turn)
        self.ticks = self.period + self.nch + self.end
        assert self.a == self.b and self.a * self.b * self.m == n


class Here:
    def __init__(self, p, swapped):
        self.p, self.swapped = p, swapped
        me = lax.axis_index("tile")
        self.mate = lax.rem(me, p.m)
        low = lax.rem(me // p.m, p.b)
        far = me // (p.m * p.b)
        self.first = far + swapped * (low - far)
        self.last = low + swapped * (far - low)
        self.first_stride = p.m * (p.b + swapped * (1 - p.b))
        self.last_stride = p.m * (1 + swapped * (p.b - 1))

    def at(self, first=0, last=0, mate=0):
        p = self.p
        f = lax.rem(self.first + (first + p.a), p.a)
        w = lax.rem(self.last + (last + p.b), p.b)
        i = lax.rem(self.mate + (mate + p.m), p.m)
        return f * self.first_stride + w * self.last_stride + i

    def near_of_source(self, off):
        return off if off == 0 else off + self.swapped * (self.p.a - 1)

    def near_of_target(self, off):
        return self.p.b - off + (1 - self.swapped) * (self.p.a - 1)


def remote(src, dst, send, recv, tile):
    return pltpu.make_async_remote_copy(
        src_ref=src,
        dst_ref=dst,
        send_sem=send,
        recv_sem=recv,
        device_id={"tile": tile},
        device_id_type=MESH,
    )


def landed(ref, sem):
    pltpu.make_async_copy(ref, ref, sem).wait()


class Swap:
    def __init__(self, p, here, edges, rows, bufs, sems, meta):
        self.p, self.here, self.edges, self.rows, self.meta = p, here, edges, rows, meta
        self.raw, self.s2, self.r2, self.s3, self.r3 = bufs
        self.send, self.recv = sems
        p = self.p

    def first(self, u, off):
        return remote(
            self.raw.at[u, 0], self.raw.at[u, off], self.send.at[0, off],
            self.recv.at[u, 0], self.here.at(first=off),
        )

    def own_slots(self, u, off):
        return remote(
            self.s2.at[u, off - 1, 0], self.r2.at[u, off - 1, 0], self.send.at[1, 0],
            self.recv.at[u, 1], self.here.at(mate=off),
        )

    def far_slots(self, u, off):
        part = pl.ds(1, self.p.a - 1)
        return remote(
            self.s2.at[u, off - 1, part], self.r2.at[u, off - 1, part], self.send.at[1, 0],
            self.recv.at[u, 1], self.here.at(mate=off),
        )

    def last(self, u, off):
        return remote(
            self.s3.at[u, off - 1], self.r3.at[u, off - 1], self.send.at[2, 0],
            self.recv.at[u, 2], self.here.at(last=off),
        )

    def wanted(self, which, edge):
        return jnp.broadcast_to(self.meta[which, pl.ds(edge, 1), :], (8, C))

    def fill(self, u, source):
        p, here = self.p, self.here
        rows = [self.wanted(here.near_of_source(source), src) for _, src in self.edges]
        index = [j for j in range(len(self.edges))]
        slot_of = {src: j for j, (_, src) in enumerate(sorted(self.edges, key=lambda x: x[1]))}
        for off in range(1, p.m):
            for low in range(p.b):
                dest = here.at(last=low, mate=off)
                masks = [row == dest for row in rows]
                for d in range(self.rows // 8):
                    part = pl.ds(8 * d, 8)
                    value = None
                    for j in index:
                        strip = self.raw[u, source, slot_of[self.edges[j][1]], part, :]
                        value = strip if value is None else jnp.where(masks[j], strip, value)
                    self.s2[u, off - 1, source, low, part, :] = value

    def start(self, u):
        p = self.p
        for off in range(1, p.a):
            self.first(u, off).start()
        self.fill(u, 0)
        for off in range(1, p.m):
            self.own_slots(u, off).start()

    def middle(self, u):
        p = self.p
        landed(self.raw.at[u, pl.ds(1, p.a - 1)], self.recv.at[u, 0])
        for off in range(1, p.a):
            self.fill(u, off)
        for off in range(1, p.m):
            self.far_slots(u, off).start()

    def arrived(self, u, low, which):
        p, here = self.p, self.here
        slot_of = {src: j for j, (_, src) in enumerate(sorted(self.edges, key=lambda x: x[1]))}
        result = []
        for j, (dst, src) in enumerate(self.edges):
            want = self.wanted(which, dst)
            sources = []
            for far in range(p.a):
                if low or far:
                    ident = here.at(first=-far)
                    sources.append((want == ident, lambda part, far=far, slot=slot_of[src]: self.raw[u, far, slot, part, :]))
                for off in range(1, p.m):
                    ident = here.at(first=-far, mate=-off)
                    sources.append(
                        (want == ident, lambda part, far=far, off=off: self.r2[u, off - 1, far, low, part, :])
                    )
            result.append((want, sources))
        return result

    def late(self, u):
        p, here = self.p, self.here
        landed(self.r2.at[u], self.recv.at[u, 1])
        for low in range(1, p.b):
            for j, (_, sources) in enumerate(self.arrived(u, low, here.near_of_target(low))):
                for d in range(self.rows // 8):
                    part = pl.ds(8 * d, 8)
                    value = None
                    for mask, load in sources:
                        value = load(part) if value is None else jnp.where(mask, load(part), value)
                    self.s3[u, low - 1, j, part, :] = value
            self.last(u, low).start()

    def finish(self, u):
        p, here = self.p, self.here
        landed(self.r3.at[u], self.recv.at[u, 2])
        strips = []
        for j, (want, sources) in enumerate(self.arrived(u, 0, 0)):
            for off in range(1, p.b):
                column = self.column(want)
                ident = lax.rem(here.last + (p.b - off), p.b)
                sources.append((column == ident, lambda part, off=off: self.r3[u, off - 1, j, part, :]))
            for d in range(self.rows // 8):
                part = pl.ds(8 * d, 8)
                value = None
                for mask, load in sources:
                    value = load(part) if value is None else jnp.where(mask, load(part), value)
                strips.append(value)
        return strips

    def column(self, want):
        p, here = self.p, self.here
        near, far = lax.rem(lax.div(want, p.m), p.b), lax.div(want, p.m * p.b)
        return near + here.swapped * (far - near)

    def drain(self):
        p = self.p
        for off in range(1, p.a):
            landed(self.raw.at[:, 0], self.send.at[0, off])
        landed(self.s2, self.send.at[1, 0])
        landed(self.s3, self.send.at[2, 0])


def reversed_lanes(x):
    row = lax.broadcasted_iota(jnp.int32, (C, C), 0)
    col = lax.broadcasted_iota(jnp.int32, (C, C), 1)
    turn = jnp.where(row + col == C - 1, 1.0, 0.0).astype(jnp.bfloat16)
    pieces = []
    for _ in range(3):
        pieces.append(x.astype(jnp.bfloat16))
        x = x - pieces[-1].astype(jnp.float32)
    return jnp.dot(
        jnp.concatenate(pieces, 1),
        jnp.concatenate([turn] * 3, 0),
        preferred_element_type=jnp.float32,
    )


def kernel(
    p, near_in, flips_in, roots_in, q_in, cour, diff, out,
    q, qt, xs, fields, fpad, coef, meta,
    raw, s2, r2, s3, r3, fraw, fs2, fr2, fs3, fr3,
    send, recv, fsend, frecv, in_sem, field_sem, spread_sem, meta_sem, table_sem,
    near, flips, roots,
):
    here = Here(p, 0)
    spec = lax.axis_index("spec")
    sc, nch = p.sc, p.nch

    def plane_in(c, s):
        return pltpu.make_async_copy(
            q_in.at[(c // 2) * sc + s, lax.rem(c, 2)],
            q.at[c, pl.ds(s * PITCH + 8, C), :],
            in_sem.at[c],
        )

    barrier = pltpu.get_barrier_semaphore()
    partners = [here.at(first=o) for o in range(1, p.a)]
    partners += [here.at(mate=o) for o in range(1, p.m)]
    partners += [here.at(last=o) for o in range(1, p.b)]
    for tile in partners:
        pl.semaphore_signal(barrier, inc=1, device_id={"tile": tile}, device_id_type=MESH)
    for off in range(1, p.members):
        peer = lax.rem(spec + off, p.members)
        pl.semaphore_signal(barrier, inc=1, device_id={"spec": peer}, device_id_type=MESH)

    tables = [
        pltpu.make_async_copy(src, dst, table_sem.at[i])
        for i, (src, dst) in enumerate(((near_in, near), (flips_in, flips), (roots_in, roots)))
    ]
    for copy in tables:
        copy.start()

    def planes_in(c):
        for s in range(sc):
            plane_in(c, s).start()

    planes_in(0)
    own_fields = [
        pltpu.make_async_copy(src.at[0], fields.at[t, spec], field_sem.at[t])
        for t, src in enumerate((cour, diff))
    ]
    for copy in tables:
        copy.wait()
    edge_row = lax.broadcasted_iota(jnp.int32, (8, C), 0)
    tile = jnp.full((8, C), near[0, 3], jnp.int32)
    for e in range(3):
        tile = jnp.where(edge_row == e, near[0, e], tile)
    meta[0] = tile

    def spread(t, src, off):
        peer = lax.rem(spec + off, p.members)
        return pltpu.make_async_remote_copy(
            src_ref=src.at[0],
            dst_ref=fields.at[t, spec],
            send_sem=spread_sem.at[0, t, off - 1],
            recv_sem=spread_sem.at[1, t, off - 1],
            device_id={"spec": peer},
            device_id_type=MESH,
        )

    spreads = [
        spread(t, src, off) for off in range(1, p.members) for t, src in enumerate((cour, diff))
    ]
    metas = []
    for way in range(2):
        for o in range(1, p.a):
            i = way * (p.a - 1) + o
            to = here.at(last=o) if way else here.at(first=o)
            metas.append(remote(meta.at[0], meta.at[i], meta_sem.at[0, i - 1], meta_sem.at[1, i - 1], to))

    def data_of(c):
        return Swap(
            p, Here(p, 1 - lax.rem(c, 2)), DATA_EDGES, 24, (raw, s2, r2, s3, r3), (send, recv), meta
        )

    face = Swap(p, here, FACE_EDGES, 8, (fraw, fs2, fr2, fs3, fr3), (fsend, frecv), meta)

    def transpose_planes(src, dst):
        for s in range(sc):
            rows = pl.ds(s * PITCH + 8, C)
            dst[rows, :] = src[rows, :].T

    def pack(u):
        strips = []
        for ref, first in ((qt, 0), (qt, C - 1), (q, 0), (q, C - 1)):
            for d in range(3):
                at = first + d if first == 0 else first - d
                strip = ref[u, pl.ds(8 + at, sc, stride=PITCH), :]
                if sc < 8:
                    strip = jnp.concatenate([strip, jnp.zeros((8 - sc, C), jnp.float32)], 0)
                strips.append(strip)
        turned = reversed_lanes(jnp.concatenate(strips, 0))
        for e in range(4):
            flipped = jnp.full((8, C), flips[0, e], jnp.int32) == 1
            for d in range(3):
                i = 3 * e + d
                raw[u, 0, e, pl.ds(8 * d, 8), :] = jnp.where(
                    flipped, turned[8 * i : 8 * i + 8], strips[i]
                )

    def prepare_fields():
        for copy in own_fields:
            copy.wait()
        for copy in spreads:
            copy.wait_recv()
        for t in range(2):
            for k in range(2):
                root = roots[0, k]
                for lev in range(2):
                    at = ((k * 2 + t) * 2 + lev) * FPITCH
                    fpad[0, pl.ds(at, C), :] = fields[t, root, k, 0, lev].T
                    fpad[1, pl.ds(at, C), :] = fields[t, root, k, 1, lev]

    def pack_faces():
        for i, e in enumerate((0, 2)):
            tile = fpad[i, pl.ds(0, 8, stride=FPITCH), :]
            flipped = jnp.full((8, C), flips[0, e], jnp.int32) == 1
            fraw[0, 0, i] = jnp.where(flipped, reversed_lanes(tile), tile)

    def end_faces():
        for i, tile in enumerate(face.finish(0)):
            fpad[i, pl.ds(C, 8, stride=FPITCH), :] = tile

    def coefficients(k, r):
        at = pl.multiple_of(r * 8, 8)
        for lev in range(2):
            for way in range(2):
                low, high = [], []
                for t in range(2):
                    base = ((k * 2 + t) * 2 + lev) * FPITCH + at
                    low.append(fpad[way, pl.ds(pl.multiple_of(base, 8), 8), :])
                    high.append(fpad[way, pl.ds(base + 1, 8), :])
                values = stencil(taps(*low), taps(*high))
                if way == 1:
                    values[3] = values[3] + 1.0
                for i, value in enumerate(values):
                    coef[k * 2 + lev, way * 7 + i, pl.ds(at, 8), :] = value

    def stencil_rows(k, c, way, src, dst, r):
        at = pl.multiple_of(r * 8, 8)
        which = k * 2 + lax.rem(c, 2)
        w = [coef[which, way * 7 + i, pl.ds(at, 8), :] for i in range(7)]
        for s in range(sc):
            row = s * PITCH + 8 + at
            total = None
            for i, d in enumerate(SHIFTS):
                term = w[i] * src[pl.ds(row + d, 8), :]
                total = term if total is None else total + term
            dst[pl.ds(pl.multiple_of(row, 8), 8), :] = total

    def interior(k, c):
        u = k * nch + c

        @pl.loop(1, C // 8 - 1)
        def _(r):
            stencil_rows(k, c, 0, qt.at[u], xs.at[c], r)

        @pl.loop(1, C // 8 - 1)
        def _(r):
            stencil_rows(k, c, 1, q.at[u], q.at[u + nch], r)

    def complete(k, c):
        u = k * nch + c
        here_q, here_t, next_q = q.at[u], qt.at[u], q.at[u + nch]
        strips = data_of(c).finish(u)
        for e, (ref, low) in enumerate(
            ((here_t, True), (here_t, False), (here_q, True), (here_q, False))
        ):
            for d in range(3):
                at = 7 - d if low else C + 8 + d
                ref[pl.ds(at, sc, stride=PITCH), :] = strips[3 * e + d][:sc]
        for r in (0, C // 8 - 1):
            stencil_rows(k, c, 0, here_t, xs.at[c], r)
            stencil_rows(k, c, 1, here_q, next_q, r)

    def joined(k, c, s):
        rows = pl.ds(s * PITCH + 8, C)
        return q[(k + 1) * nch + c, rows, :] + xs[c, rows, :].T

    def staged(t, delay):
        at = t - delay
        k = at // p.period
        c = at - k * p.period
        return k, c, (at >= 0) & (k < 2) & (c < nch)

    @pl.loop(0, nch)
    def _(c):
        @pl.when(c + 1 < nch)
        def _():
            planes_in(c + 1)

        landed(q.at[c, pl.ds(0, sc * C), :], in_sem.at[c])
        transpose_planes(q.at[c], qt.at[c])
        pack(c)

        @pl.when(c == 0)
        def _():
            pl.semaphore_wait(barrier, len(partners) + p.members - 1)

        data_of(c).start(c)

        @pl.when(c == 0)
        def _():
            for copy in metas + spreads + own_fields:
                copy.start()

    prepare_fields()
    pack_faces()
    face.start(0)

    @pl.loop(0, C // 8 - 1)
    def _(r):
        coefficients(0, r)
        coefficients(1, r)

    for copy in metas:
        copy.wait_recv()

    def do_late(t):
        k, c, on = staged(t, p.late)

        @pl.when(on)
        def _():
            data_of(c).late(k * nch + c)

        @pl.when(t == p.face_late)
        def _():
            face.late(0)

    def do_middle(t):
        k, c, on = staged(t, 0)

        @pl.when(on)
        def _():
            data_of(c).middle(k * nch + c)

        @pl.when(t == p.face_middle)
        def _():
            face.middle(0)

    def do_interior(t):
        @pl.when(t < nch)
        def _():
            interior(0, t)

    def do_end(t):
        @pl.when(t == p.end)
        def _():
            end_faces()
            coefficients(0, C // 8 - 1)
            coefficients(1, C // 8 - 1)

        k, c, on = staged(t, p.end)

        @pl.when(on)
        def _():
            complete(k, c)

            @pl.when(k == 0)
            def _():
                for s in range(sc):
                    rows = pl.ds(s * PITCH + 8, C)
                    plane = joined(0, c, s)
                    q[nch + c, rows, :] = plane
                    qt[nch + c, rows, :] = plane.T
                pack(nch + c)
                data_of(c).start(nch + c)
                interior(1, c)

            @pl.when(k == 1)
            def _():
                for s in range(sc):
                    out[(c // 2) * sc + s, lax.rem(c, 2)] = joined(1, c, s)

    @pl.loop(0, p.ticks)
    def _(t):
        for part in (do_middle, do_late, do_interior, do_end):
            part(t)

    for copy in metas + spreads:
        copy.wait_send()
    face.drain()
    data_of(0).drain()


def body(sizes, tracers, courant, diffusivity, edge_blocks, edge_flips, roots):
    p = Plan(sizes, tracers.shape[0])
    anywhere = pl.BlockSpec(memory_space=pl.ANY)
    f32 = jnp.float32

    def buffers(nu, edges, rows):
        return [
            pltpu.VMEM((nu, p.a, edges, rows, C), f32),
            pltpu.VMEM((nu, p.m - 1, p.a, p.b, rows, C), f32),
            pltpu.VMEM((nu, p.m - 1, p.a, p.b, rows, C), f32),
            pltpu.VMEM((nu, p.b - 1, edges, rows, C), f32),
            pltpu.VMEM((nu, p.b - 1, edges, rows, C), f32),
        ]

    dma = pltpu.SemaphoreType.DMA
    return pl.pallas_call(
        functools.partial(kernel, p),
        out_shape=pltpu.VMEM(tracers.shape, tracers.dtype),
        in_specs=[anywhere] * 6,
        out_specs=pl.BlockSpec(memory_space=pltpu.VMEM),
        scratch_shapes=[
            pltpu.VMEM((3 * p.nch, p.sc * PITCH, C), f32),
            pltpu.VMEM((2 * p.nch, p.sc * PITCH, C), f32),
            pltpu.VMEM((p.nch, p.sc * PITCH, C), f32),
            pltpu.VMEM((2, p.members, 2, 2, 2, C, C), f32),
            pltpu.VMEM((2, 8 * FPITCH, C), f32),
            pltpu.VMEM((4, 14, C, C), f32),
            pltpu.VMEM((p.a + p.b - 1, 8, C), jnp.int32),
            *buffers(p.nu, 4, 24),
            *buffers(1, 2, 8),
            dma((3, p.a)),
            dma((p.nu, 3)),
            dma((3, p.a)),
            dma((1, 3)),
            dma((p.nch,)),
            dma((2,)),
            dma((2, 2, p.members - 1)),
            dma((2, p.a + p.b - 2)),
            dma((3,)),
            pltpu.SMEM((1, 4), jnp.int32),
            pltpu.SMEM((1, 4), jnp.int32),
            pltpu.SMEM((1, 2), jnp.int32),
        ],
        compiler_params=pltpu.CompilerParams(
            collective_id=0, has_side_effects=True, vmem_limit_bytes=VMEM_LIMIT
        ),
        name="transport",
    )(edge_blocks, edge_flips, roots.reshape(1, 2), tracers, courant, diffusivity)


def solution(mesh):
    placed = (
        P("spec", None, "tile", None),
        P("spec", None, None, None, "tile", None),
        P("spec", None, None, None, "tile", None),
        P("tile", None),
        P("tile", None),
        P(None, "tile"),
    )
    return jax.shard_map(
        functools.partial(body, dict(mesh.shape)),
        mesh=mesh,
        in_specs=placed,
        out_specs=P("spec", None, "tile", None),
        check_vma=False,
    )
```
